256 devices in a mesh: grp: 8 (over y, core), dev: 32 (over x, z).
Axes of the slice: x: 4, y: 4, z: 8, core: 2. Of those that a mesh axis runs over, the one named last changes fastest.
Arguments:
- conc_old: float32 [256, 1024, 256], P('grp', 'dev'), may hold values from 0.5 to 2
- phi_old: float32 [256, 1024, 256], P('grp', 'dev'), may hold values from -6 to 6
- solid_pot: float32 [256, 1024, 256], P('grp', 'dev'), may hold values from -4.5 to 6
- phase_label: int32 [256, 1024, 256], P('grp', 'dev'), may hold values from 0 to 2
- iface_block: int32 [8, 8192], P('grp', 'dev'), may hold values from 0 to 2047
- iface_owner: int32 [8, 8192, 1], P('grp', 'dev'), may hold values from 0 to 31; in each aligned block of 256 rows (0 to 255, 256 to 511, ..., all dimensions but the last counted through in order) at most 16 rows name the same one
Outputs:
- concentration: float32 [256, 1024, 256], P('grp', 'dev')
- flux: float32 [256, 1024, 256], P('grp', 'dev')
- potential: float32 [256, 1024, 256], P('grp', 'dev')
The draws below stay inside these ranges and needn't reach their ends.
Inputs may be any that keep to these rules, and one draw needn't show every extreme that they name: `iface_owner`: among the 256 entries of one index of dev, no owner is named more than 16 times, a bound that some block reaches.
All inputs are finite; a program needn't handle non-finite values.
Results may differ from the reference program's by a relative error of at most 0.0005.
Values sent between devices are 32-bit elements; how exact they have to be, the bound alone decides.
A program may use at most 64 MiB of HBM per device.

```python
import math
import jax
import jax.numpy as jnp
import numpy as np

CX = 32
CY = 32
CZ = 256
LIST_DEV = 256
SWEEPS = 4
SMOOTH = 2
COARSE_SWEEPS = 8
GROUPS = 8
NX = 256
NY = 1024
BLK_DEV = 2048
CAP = 16
LIST = 8192
N_DEV = 32


def brick_offsets(key):
    table_key = jax.random.fold_in(key, 7301)
    table_off = jax.random.uniform(table_key, (NX // CX, NY // CY), jnp.float32, -4.0, 4.0)
    spread_off = jnp.repeat(jnp.repeat(table_off, CX, axis=0), CY, axis=1)
    return spread_off[:, :, None]


def draw_phi_old(key, part):
    rough_key = jax.random.fold_in(key, 4111)
    rough = jnp.clip(jax.random.normal(rough_key, (NX, NY, CZ), jnp.float32), -2.0, 2.0)
    return (brick_offsets(key) + rough).astype(jnp.float32)


def draw_solid_pot(key, part):
    rough_key = jax.random.fold_in(key, 5923)
    unit = jax.random.uniform(rough_key, (NX, NY, CZ), jnp.float32, 0.0, 1.0)
    rough = -0.5 + 2.5 * unit
    return (brick_offsets(key) + rough).astype(jnp.float32)


def with_ends(values, stream_key, smallest, top_value):
    longest = values.shape.index(max(values.shape))
    spots = []
    for shift in (0, 1):
        where = [jax.random.randint(jax.random.fold_in(stream_key, axis), (), 0, length) for axis, length in enumerate(values.shape)]
        where[longest] = (where[longest] + shift) % values.shape[longest]
        spots.append(tuple(where))
    return values.at[spots[0]].set(smallest).at[spots[1]].set(top_value)


def level_of(rng, shape, split, low, top_value):
    def one(dim, shards_of):
        draws = jax.random.uniform(jax.random.fold_in(jax.random.fold_in(rng, 6), dim), (shards_of,), jnp.float32, low / len(split), top_value / len(split))
        return jnp.repeat(jnp.exp(draws), shape[dim] // shards_of).reshape((-1,) + (1,) * (len(shape) - dim - 1))

    level = one(*split[0])
    for cut in split[1:]:
        level = level * one(*cut)
    return level


def deal_out(own_key, own, number, rows, count, top, reach, skew):
    sequence = jax.random.permutation(own_key, count)
    crowded, common = portions_of(count, rows * top, reach, skew, True), portions_of(count, rows * top, reach, skew, False)
    places = jnp.arange(count)

    def named(lengths, offset_by):
        used = int((lengths > 0).sum())
        fixed = max(1, used // 4)
        moved = fixed + (places - fixed + offset_by * (used - fixed)) % max(1, count - fixed)
        return jnp.zeros((count,), jnp.int32).at[sequence[jnp.where(places < fixed, places, moved)]].set(jnp.asarray(lengths, jnp.int32))

    lengths = jnp.where(number % 4 == 0, named(crowded, number // 4), named(common, number - number // 4 - 1))
    mixed = jax.random.permutation(jax.random.fold_in(own, 3), count)
    source_of, taker = mixed[0:count // 2 * 2:2], mixed[1:count // 2 * 2:2]
    room = jnp.minimum(lengths[source_of] - 1, reach - lengths[taker]) // 2
    room = jnp.where((source_of == sequence[0]) | (taker == sequence[0]) | (lengths[taker] == 0), 0, jnp.maximum(room, 0))
    moved = jax.random.randint(jax.random.fold_in(own, 4), (count // 2,), 0, 1 << 20) % (room + 1)
    lengths = lengths.at[source_of].add(-moved).at[taker].add(moved)
    items = jnp.searchsorted(jnp.cumsum(lengths), jnp.arange(rows * top), side="right").astype(jnp.int32)
    grid = items.reshape(top, rows).T
    grid = grid[jax.random.permutation(jax.random.fold_in(own, 1), rows)]
    offset_by = jax.random.randint(jax.random.fold_in(own, 2), (rows, 1), 0, top)
    return jnp.take_along_axis(grid, (jnp.arange(top)[None, :] + offset_by) % top, axis=1)


def portions_of(count, total, bound, skew, full):
    portions = [(1 << 20) // math.isqrt(grade ** skew) + 1 for grade in range(1, count + 1)]
    largest = bound if full else min(bound, max(-(-total // count), total * portions[0] // sum(portions)))
    least = 1 if total - largest >= count - 1 else 0
    counts, rest = [largest] + [least] * (count - 1), total - largest - least * (count - 1)
    while rest > 0:
        candidates = [i for i in range(1, count) if counts[i] < largest] or [i for i in range(1, count) if counts[i] < bound]
        pool, remaining = sum([portions[i] for i in candidates]), rest
        for i in candidates:
            addition = min(bound - counts[i], max(1, remaining * portions[i] // pool), rest)
            counts[i] = counts[i] + addition
            rest = rest - addition
    return np.array(counts)


def setup_inputs(seed: int = 0) -> dict:
    key_list = jax.random.split(jax.random.key(seed), 7)
    conc_old = jnp.clip(jnp.exp(math.log(2.0) - 1.3862944 * jax.random.uniform(key_list[0], (NX, NY, CZ), jnp.float32) ** level_of(key_list[0], (NX, NY, CZ), ((0, 8), (1, 32)), -0.2, 0.2)), 0.5, 2.0)
    phi_old = draw_phi_old(jax.random.fold_in(key_list[6], 71), 0)
    solid_pot = draw_solid_pot(jax.random.fold_in(key_list[6], 71), 0)
    phase_label = with_ends(jax.random.randint(key_list[3], (NX, NY, CZ), 0, 3), jax.random.fold_in(key_list[3], 1), 0, 2).astype(jnp.int32)
    iface_block = with_ends(jax.random.randint(key_list[4], (GROUPS, LIST), 0, BLK_DEV), jax.random.fold_in(key_list[4], 1), 0, BLK_DEV - 1).astype(jnp.int32)
    iface_owner_keys = jax.random.split(jax.random.fold_in(key_list[5], 1), GROUPS * LIST // LIST_DEV)
    iface_owner_turns = jax.random.permutation(jax.random.fold_in(key_list[5], 3), GROUPS * LIST // LIST_DEV)
    iface_owner = jax.vmap(lambda own, number: deal_out(jax.random.fold_in(key_list[5], 2), own, number, LIST_DEV, N_DEV, 1, CAP, 2))(iface_owner_keys, iface_owner_turns).reshape((GROUPS, LIST, 1))
    return {"conc_old": conc_old, "phi_old": phi_old, "solid_pot": solid_pot, "phase_label": phase_label, "iface_block": iface_block, "iface_owner": iface_owner}


MASS = 0.05
OMEGA = 0.8
DIFFUSION_TABLE = (1.5, 0.1, 0.4)
CONDUCT_TABLE = (1.0, 0.3, 0.6)
KINETIC_TABLE = (0.2, 1.0, 0.5)

def lookup(phase_label, table_vals):
    return jnp.where(phase_label == 0, table_vals[0], jnp.where(phase_label == 1, table_vals[1], table_vals[2])).astype(jnp.float32)

def split_parts(padded):
    middle = padded[1:-1, 1:-1, 1:-1]
    in_plane = padded[2:, 1:-1, 1:-1] + padded[:-2, 1:-1, 1:-1] + padded[1:-1, 2:, 1:-1] + padded[1:-1, :-2, 1:-1]
    along_z = padded[1:-1, 1:-1, 2:] + padded[1:-1, 1:-1, :-2]
    return (middle, in_plane, along_z)

def apply_level(padded, conduct, weight):
    middle, in_plane, along_z = split_parts(padded)
    return MASS * middle + conduct * (weight * (4.0 * middle - in_plane) + 2.0 * middle - along_z)

def zero_padded(field_in):
    return jnp.pad(field_in, 1)

def smooth(current, source, conduct, weight, padder):
    diagonal = MASS + conduct * (4.0 * weight + 2.0)
    return current + OMEGA * (source - apply_level(padder(current), conduct, weight)) / diagonal

def residual_of(current, source, conduct, weight, padder):
    return source - apply_level(padder(current), conduct, weight)

def restrict(field_in):
    extent_x, extent_y, extent_z = field_in.shape
    return field_in.reshape(extent_x // 2, 2, extent_y // 2, 2, extent_z).mean(axis=(1, 3))

def inject(field_in):
    return jnp.repeat(jnp.repeat(field_in, 2, axis=0), 2, axis=1)

def butler_volmer(concentration, phi_old, solid_pot, kinetic):
    over_pot = solid_pot - phi_old - 0.2 * jnp.log(concentration)
    return 2.0 * kinetic * jnp.sqrt(concentration) * jnp.sinh(0.5 * over_pot)

def coarse_solve(source, conduct):
    current = jnp.zeros_like(source)
    for _ in range(COARSE_SWEEPS):
        current = smooth(current, source, conduct, 0.0625, zero_padded)
    resid_coarse = residual_of(current, source, conduct, 0.0625, zero_padded)
    load = apply_level(zero_padded(jnp.ones_like(source)), conduct, 0.0625)
    return current + jnp.sum(resid_coarse) / jnp.sum(load)

def reference(conc_old, phi_old, solid_pot, phase_label, iface_block, iface_owner):
    diffusion = lookup(phase_label, DIFFUSION_TABLE)
    concentration = conc_old
    for _ in range(SWEEPS):
        middle, in_plane, along_z = split_parts(zero_padded(concentration))
        concentration = (conc_old + diffusion * (in_plane + along_z)) / (1.0 + 6.0 * diffusion)
    kinetic = lookup(phase_label, KINETIC_TABLE)
    flux_all = butler_volmer(concentration, phi_old, solid_pot, kinetic)
    owners = iface_owner[:, :, 0]
    group_ids = jnp.broadcast_to(jnp.arange(GROUPS, dtype=jnp.int32)[:, None], owners.shape)
    listed = jnp.zeros((GROUPS, N_DEV, BLK_DEV), jnp.float32).at[group_ids, owners, iface_block].set(1.0)
    listed = listed.reshape(GROUPS, N_DEV, CX, CY, CZ // 128).transpose(0, 2, 1, 3, 4).reshape(NX, NY, CZ // 128)
    flux = (flux_all.reshape(NX, NY, CZ // 128, 128) * listed[..., None]).reshape(NX, NY, CZ)
    conduct = lookup(phase_label, CONDUCT_TABLE) * conc_old
    source_fine = MASS * phi_old + flux
    potential = phi_old
    for _ in range(SMOOTH):
        potential = smooth(potential, source_fine, conduct, 1.0, zero_padded)
    resid_fine = residual_of(potential, source_fine, conduct, 1.0, zero_padded)
    conduct_mid = restrict(conduct)
    source_mid = restrict(resid_fine)
    error_mid = jnp.zeros_like(source_mid)
    for _ in range(SMOOTH):
        error_mid = smooth(error_mid, source_mid, conduct_mid, 0.25, zero_padded)
    resid_mid = residual_of(error_mid, source_mid, conduct_mid, 0.25, zero_padded)
    conduct_coarse = restrict(conduct_mid).reshape(GROUPS, CX // 4, NY // 4, CZ)
    source_coarse = restrict(resid_mid).reshape(GROUPS, CX // 4, NY // 4, CZ)
    error_coarse = jax.vmap(coarse_solve)(source_coarse, conduct_coarse)
    error_coarse = error_coarse.reshape(NX // 4, NY // 4, CZ)
    error_mid = error_mid + inject(error_coarse)
    for _ in range(SMOOTH):
        error_mid = smooth(error_mid, source_mid, conduct_mid, 0.25, zero_padded)
    potential = potential + inject(error_mid)
    for _ in range(SMOOTH):
        potential = smooth(potential, source_fine, conduct, 1.0, zero_padded)
    return (concentration, flux, potential)
```

```python
import functools

import jax
import jax.numpy as jnp
from jax import lax
from jax.experimental import pallas as pl
from jax.experimental.pallas import tpu as pltpu
from jax.sharding import PartitionSpec as P

MESH = pl.DeviceIdType.MESH
F32 = jnp.float32

FX, FY = 40, 48
MX, MY = 24, 32
EX, EY = 16, 24
GX, GY = 10, 40


def lookup(label, table):
    return jnp.where(label == 0, table[0], jnp.where(label == 1, table[1], table[2])).astype(F32)


def kernel(
    n_grp,
    n_dev,
    conc_hbm,
    phi_hbm,
    solid_hbm,
    label_hbm,
    lists_ref,
    conc_out,
    flux_out,
    pot_out,
    c0, lb, ph, sp, ca, cb, dd, cc, kk, gg, qq, bb, fx, p2,
    sm, km, gm, bm, m1, m2,
    kc, rc, gc, wa, wb, ka, kb, sc, ea, eb,
    ec,
    ysf, yrf, ysl, yrl, ysm, yrm, yse, yre,
    lrecv, msk, psend, precv,
    in_sem, out_sem, hs_sem, hr_sem, cs_sem, cr_sem, ls_sem, lr_sem, ps_sem, pr_sem,
):
    g = lax.axis_index("grp")
    d = lax.axis_index("dev")
    gu, gd = lax.rem(g + 1, n_grp), lax.rem(g + n_grp - 1, n_grp)
    du, dl = lax.rem(d + 1, n_dev), lax.rem(d + n_dev - 1, n_dev)
    eight = [(gd, dl), (gd, d), (gd, du), (g, dl), (g, du), (gu, dl), (gu, d), (gu, du)]
    lane = lax.broadcasted_iota(jnp.int32, (1, 128), 1)
    l0, l1 = lane == 0, lane == 127

    loads = []
    for k, (src, dst) in enumerate(((conc_hbm, c0), (label_hbm, lb), (phi_hbm, ph))):
        for h in range(2):
            loads.append(
                pltpu.make_async_copy(
                    src.at[:, :, pl.ds(128 * h, 128)], dst.at[pl.ds(4, 32), h, pl.ds(8, 32), :], in_sem.at[2 * k + h]
                )
            )
    for h in range(2):
        loads.append(
            pltpu.make_async_copy(solid_hbm.at[:, :, pl.ds(128 * h, 128)], sp.at[:, h], in_sem.at[6 + h])
        )
    for load in loads:
        load.start()

    barrier = pltpu.get_barrier_semaphore()
    for t in (eight[0], eight[1], eight[2], eight[5], eight[6], eight[7]):
        pl.semaphore_signal(barrier, inc=1, device_id=t, device_id_type=MESH)

    def greet(j, carry):
        pl.semaphore_signal(barrier, inc=1, device_id=(g, lax.rem(d + j, n_dev)), device_id_type=MESH)
        return carry

    lax.fori_loop(1, n_dev, greet, 0)

    for ref, rows in ((kc, (0, 8, 32, 40)), (sc, (0, 8, 32, 40)), (ka, (0, 8, 32, 40)), (kb, (0, 8, 32, 40)), (ea, (0, 8, 32, 40)), (eb, (0, 8, 32, 40))):
        ref[:, :, 0:8, :] = jnp.zeros((GX, 2, 8, 128), F32)
        ref[:, :, 32:40, :] = jnp.zeros((GX, 2, 8, 128), F32)
        ref[0] = jnp.zeros((2, GY, 128), F32)
        ref[GX - 1] = jnp.zeros((2, GY, 128), F32)
    lrecv[d] = lists_ref[...]

    def pack(field, ys, n):
        def one(i, carry):
            for s, r in ((0, 8), (1, 8 + n - 4)):
                for h in range(2):
                    ys[s, i, h, 0:4, :] = field[4 + 2 * i, h, r : r + 4, :]
                    ys[s, i, h, 4:8, :] = field[5 + 2 * i, h, r : r + 4, :]
            return carry

        lax.fori_loop(0, n // 2, one, 0, unroll=4)

    def unpack(field, yr, n, zero):
        def one(i, carry):
            for s, r, edge in ((0, 4, d == 0), (1, 8 + n, d == n_dev - 1)):
                for h in range(2):
                    v = jnp.where(edge, jnp.zeros((8, 128), yr.dtype), yr[s, i, h])
                    field[2 * i, h, r : r + 4, :] = v[0:4]
                    field[2 * i + 1, h, r : r + 4, :] = v[4:8]
            return carry

        lax.fori_loop(0, n // 2 + 4, one, 0, unroll=4)
        if zero:
            @pl.when(g == 0)
            def _():
                field[0:4] = jnp.zeros(field.at[0:4].shape, field.dtype)

            @pl.when(g == n_grp - 1)
            def _():
                field[4 + n : 8 + n] = jnp.zeros(field.at[0:4].shape, field.dtype)

    def halo(e, field, ys, yr, n):
        m = n // 2
        own = pl.ds(8, n)
        low, high = field.at[pl.ds(4, 4), :, own, :], field.at[pl.ds(n, 4), :, own, :]
        to_low, to_high = field.at[pl.ds(0, 4), :, own, :], field.at[pl.ds(4 + n, 4), :, own, :]
        pairs = [
            (ys.at[0, pl.ds(0, 2)], yr.at[1, pl.ds(m + 2, 2)]),
            (low, to_high),
            (ys.at[1, pl.ds(0, 2)], yr.at[0, pl.ds(m + 2, 2)]),
            (ys.at[0], yr.at[1, pl.ds(2, m)]),
            (ys.at[1], yr.at[0, pl.ds(2, m)]),
            (ys.at[0, pl.ds(m - 2, 2)], yr.at[1, pl.ds(0, 2)]),
            (high, to_low),
            (ys.at[1, pl.ds(m - 2, 2)], yr.at[0, pl.ds(0, 2)]),
        ]
        copies = []
        for i in (4, 3, 6, 1, 0, 2, 5, 7):
            src, dst = pairs[i]
            copies.append(
                pltpu.make_async_remote_copy(
                    src_ref=src, dst_ref=dst, send_sem=hs_sem.at[e, i], recv_sem=hr_sem.at[e, i],
                    device_id=eight[i], device_id_type=MESH,
                )
            )
        for c in copies:
            c.start()
        return copies

    def arrive(copies):
        for c in copies:
            c.wait_recv()

    def all_send(src, dst, send_sem, recv_sem):
        def one(j, carry):
            pltpu.make_async_remote_copy(
                src_ref=src, dst_ref=dst.at[d], send_sem=send_sem.at[j], recv_sem=recv_sem.at[d],
                device_id=(g, lax.rem(d + j, n_dev)), device_id_type=MESH,
            ).start()
            return carry

        lax.fori_loop(1, n_dev, one, 0)

    def all_wait(src, dst, send_sem, recv_sem):
        def one(j, carry):
            s = lax.rem(d + n_dev - j, n_dev)
            c = pltpu.make_async_remote_copy(
                src_ref=src, dst_ref=dst.at[s], send_sem=send_sem.at[j], recv_sem=recv_sem.at[s],
                device_id=(g, lax.rem(d + j, n_dev)), device_id_type=MESH,
            )
            c.wait_recv()
            c.wait_send()
            return carry

        lax.fori_loop(1, n_dev, one, 0)

    def z_sum(a, b):
        ra, rb = pltpu.roll(a, 1, 1), pltpu.roll(b, 1, 1)
        sa, sb = pltpu.roll(a, 127, 1), pltpu.roll(b, 127, 1)
        zero = jnp.zeros_like(a)
        za = jnp.where(l0, zero, ra) + jnp.where(l1, sb, sa)
        zb = jnp.where(l0, ra, rb) + jnp.where(l1, zero, sb)
        return za, zb

    def plane(field, x, h, r0, r1):
        return (field[x - 1, h, r0:r1, :] + field[x + 1, h, r0:r1, :]) + (
            field[x, h, r0 - 1 : r1 - 1, :] + field[x, h, r0 + 1 : r1 + 1, :]
        )

    def stencil(field, x, r0, r1, weight):
        a, b = field[x, 0, r0:r1, :], field[x, 1, r0:r1, :]
        za, zb = z_sum(a, b)
        pa, pb = plane(field, x, 0, r0, r1), plane(field, x, 1, r0, r1)
        if weight != 1.0:
            pa, pb = weight * pa, weight * pb
        return (a, b), (pa + za, pb + zb)

    def sweep(src, dst, gain, rhs, x0, x1, r0, r1, weight, unroll):
        def one(x, carry):
            v, s = stencil(src, x, r0, r1, weight)
            for h in range(2):
                dst[x, h, r0:r1, :] = 0.2 * v[h] + rhs[x, h, r0:r1, :] + gain[x, h, r0:r1, :] * s[h]
            return carry

        lax.fori_loop(x0, x1, one, 0, unroll=unroll)

    for k in range(4):
        loads[k].wait()
    pack(c0, ysf.at[0], 32)
    pack(lb, ysl, 32)
    loads[4].wait()
    loads[5].wait()
    pack(ph, ysf.at[1], 32)
    pl.semaphore_wait(barrier, n_dev - 1 + 6)
    all_send(lists_ref, lrecv, ls_sem, lr_sem)
    h_conc = halo(0, c0, ysf.at[0], yrf.at[0], 32)
    h_label = halo(1, lb, ysl, yrl, 32)
    h_phi = halo(2, ph, ysf.at[1], yrf.at[1], 32)

    def own_mid(i, carry):
        for h in range(2):
            total = jnp.zeros((16, 128), F32)
            for x in (0, 1):
                for r in (0, 1):
                    rows = pl.ds(8 + r, 16, stride=2)
                    total = total + lookup(lb[4 + 2 * i + x, h, rows, :], (1.0, 0.3, 0.6)) * c0[4 + 2 * i + x, h, rows, :]
            km[4 + i, h, 8:24, :] = 0.25 * total
        return carry

    lax.fori_loop(0, 16, own_mid, 0, unroll=2)
    pack(km, ysm.at[0], 16)
    h_km = halo(3, km, ysm.at[0], yrm.at[0], 16)

    def own_coarse(dst, src, off):
        def one(i, carry):
            for h in range(2):
                total = jnp.zeros((8, 128), F32)
                for x in (0, 1):
                    for r in (0, 1):
                        total = total + src[off + 2 * i + x, h, pl.ds(8 + r, 8, stride=2), :]
                dst[1 + i, h, 16:24, :] = 0.25 * total
            return carry

        lax.fori_loop(0, 8, one, 0, unroll=2)

    def coarse_exchange(field, k):
        copies = []
        for i, (t, r) in enumerate((((g, dl), 24), ((g, du), 8))):
            copies.append(
                pltpu.make_async_remote_copy(
                    src_ref=field.at[pl.ds(1, 8), :, pl.ds(16, 8), :], dst_ref=field.at[pl.ds(1, 8), :, pl.ds(r, 8), :],
                    send_sem=cs_sem.at[k, i], recv_sem=cr_sem.at[k, i], device_id=t, device_id_type=MESH,
                )
            )
        for c in copies:
            c.start()
        return copies

    def coarse_edges(field):
        @pl.when(d == 0)
        def _():
            field[:, :, 8:16, :] = jnp.zeros((GX, 2, 8, 128), F32)

        @pl.when(d == n_dev - 1)
        def _():
            field[:, :, 24:32, :] = jnp.zeros((GX, 2, 8, 128), F32)

    own_coarse(kc, km, 4)
    x_kc = coarse_exchange(kc, 0)

    arrive(h_conc)
    unpack(c0, yrf.at[0], 32, True)
    arrive(h_label)
    unpack(lb, yrl, 32, False)

    def coeffs(x, carry):
        for h in range(2):
            old = c0[x, h, 4:44, :]
            label = lb[x, h, 4:44, :]
            dif = jnp.where(old > 0.0, lookup(label, (1.5, 0.1, 0.4)), 0.0)
            inv = lookup(label, (1.0 / 10.0, 1.0 / 1.6, 1.0 / 3.4))
            dd[x, h, 4:44, :] = dif * inv
            cc[x, h, 4:44, :] = old * inv
            con = lookup(label, (1.0, 0.3, 0.6)) * old
            kk[x, h, 4:44, :] = con
            rd = 0.8 / (0.05 + 6.0 * con)
            bb[x, h, 4:44, :] = rd
            gg[x, h, 4:44, :] = rd * con
        return carry

    lax.fori_loop(0, FX, coeffs, 0, unroll=2)

    def conc_sweep(src, dst, x0, x1, r0, r1):
        def one(x, carry):
            _, s = stencil(src, x, r0, r1, 1.0)
            for h in range(2):
                dst[x, h, r0:r1, :] = cc[x, h, r0:r1, :] + dd[x, h, r0:r1, :] * s[h]
            return carry

        lax.fori_loop(x0, x1, one, 0, unroll=2)

    conc_sweep(c0, ca, 1, 39, 4, 44)
    conc_sweep(ca, cb, 2, 38, 4, 44)
    conc_sweep(cb, ca, 3, 37, 4, 44)
    conc_sweep(ca, cb, 4, 36, 8, 40)
    outs = []
    for h in range(2):
        outs.append(
            pltpu.make_async_copy(
                cb.at[pl.ds(4, 32), h, pl.ds(8, 32), :], conc_out.at[:, :, pl.ds(128 * h, 128)], out_sem.at[h]
            )
        )
    for o in outs:
        o.start()

    all_wait(lists_ref, lrecv, ls_sem, lr_sem)

    def count(s, carry):
        total = carry
        for r in range(2):
            owner, block = lrecv[s, r : r + 1, :], lrecv[s, r + 2 : r + 3, :]
            place = jnp.where(owner == d, (block & 1) * 32 + ((block >> 1) & 31), -1)
            column = block >> 6
            rows = (lax.broadcasted_iota(jnp.int32, (64, 128), 0) == place).astype(jnp.bfloat16)
            cols = (lax.broadcasted_iota(jnp.int32, (32, 128), 0) == column).astype(jnp.bfloat16)
            total = total + lax.dot_general(
                rows, cols, (((1,), (1,)), ((), ())), preferred_element_type=F32
            )
        return total

    counts = lax.fori_loop(0, n_dev, count, jnp.zeros((64, 32), F32), unroll=4)
    named = jnp.where(counts > 0.0, 1.0, 0.0).astype(jnp.bfloat16)
    spread = (
        lax.broadcasted_iota(jnp.int32, (32, 4096), 1) // 128 == lax.broadcasted_iota(jnp.int32, (32, 4096), 0)
    ).astype(jnp.bfloat16)
    msk[...] = jnp.dot(named, spread, preferred_element_type=F32)

    for k in (6, 7):
        loads[k].wait()
    for x in range(32):
        for h in range(2):
            con = cb[4 + x, h, 8:40, :]
            u = 0.5 * (sp[x, h] - ph[4 + x, h, 8:40, :]) - 0.1 * jnp.log(con)
            kin = lookup(lb[4 + x, h, 8:40, :], (0.2, 1.0, 0.5)) * jnp.sqrt(con)
            val = kin * (jnp.exp(u) - jnp.exp(-u))
            fx[4 + x, h, 8:40, :] = msk[32 * h : 32 * h + 32, 128 * x : 128 * x + 128] * val
    pack(fx, ysf.at[2], 32)
    h_flux = halo(4, fx, ysf.at[2], yrf.at[2], 32)
    for h in range(2):
        outs.append(
            pltpu.make_async_copy(
                fx.at[pl.ds(4, 32), h, pl.ds(8, 32), :], flux_out.at[:, :, pl.ds(128 * h, 128)], out_sem.at[2 + h]
            )
        )
        outs[-1].start()

    arrive(h_phi)
    unpack(ph, yrf.at[1], 32, True)

    def first(x, carry):
        v, s = stencil(ph, x, 4, 44, 1.0)
        for h in range(2):
            rd = bb[x, h, 4:44, :]
            qq[x, h, 4:44, :] = (0.2 + 0.05 * rd) * v[h] + gg[x, h, 4:44, :] * s[h]
        return carry

    lax.fori_loop(1, 39, first, 0, unroll=2)
    arrive(h_km)
    unpack(km, yrm.at[0], 16, True)
    arrive(x_kc)
    coarse_edges(kc)

    def coarse_coeffs(x, carry):
        for h in range(2):
            con = kc[x, h, 8:32, :]
            rd = 0.8 / (0.05 + 2.25 * con)
            rc[x, h, 8:32, :] = rd
            gc[x, h, 8:32, :] = rd * con
            wa[x, h, 8:32, :] = jnp.ones((24, 128), F32)
            ka[x, h, 8:32, :] = con
        return carry

    lax.fori_loop(1, 9, coarse_coeffs, 0)

    def dual(w_in, k_in, w_out, k_out):
        def one(x, carry):
            v, s = stencil(k_in, x, 8, 32, 0.0625)
            for h in range(2):
                w = w_in[x, h, 8:32, :]
                w = w - rc[x, h, 8:32, :] * (0.05 * w + 2.25 * v[h] - s[h])
                w_out[x, h, 8:32, :] = w
                k_out[x, h, 8:32, :] = kc[x, h, 8:32, :] * w
            return carry

        lax.fori_loop(1, 9, one, 0, unroll=4)

    for k in range(4):
        dual(wa, ka, wb, kb)
        dual(wb, kb, wa, ka)

    load = jnp.zeros((8, 128), F32)
    row = lax.broadcasted_iota(jnp.int32, (8, 128), 0)
    lane8 = lax.broadcasted_iota(jnp.int32, (8, 128), 1)
    edge_y = jnp.where(((row == 0) & (d == 0)) | ((row == 7) & (d == n_dev - 1)), 1.0, 0.0)
    for x in range(8):
        for h in range(2):
            edge_z = jnp.where(lane8 == 127 * h, 1.0, 0.0)
            edge_xy = edge_y + (1.0 if x in (0, 7) else 0.0)
            load = load + (0.05 + kc[1 + x, h, 16:24, :] * (0.0625 * edge_xy + edge_z))
    load = jnp.sum(load, axis=0, keepdims=True)

    arrive(h_flux)
    unpack(fx, yrf.at[2], 32, True)

    def second(x, carry):
        for h in range(2):
            rd = bb[x, h, 4:44, :]
            fl = fx[x, h, 4:44, :]
            ca[x, h, 4:44, :] = qq[x, h, 4:44, :] + rd * fl
            src = 0.05 * ph[x, h, 4:44, :] + fl
            qq[x, h, 4:44, :] = src
            bb[x, h, 4:44, :] = rd * src
        return carry

    lax.fori_loop(1, 39, second, 0, unroll=2)
    sweep(ca, p2, gg, bb, 2, 38, 4, 44, 1.0, 2)

    def resid(x, carry):
        v, s = stencil(p2, x, 8, 40, 1.0)
        for h in range(2):
            sp[x - 4, h] = qq[x, h, 8:40, :] - 0.05 * v[h] - kk[x, h, 8:40, :] * (6.0 * v[h] - s[h])
        return carry

    lax.fori_loop(4, 36, resid, 0, unroll=2)

    def down(i, carry):
        for h in range(2):
            total = jnp.zeros((16, 128), F32)
            for x in (0, 1):
                for r in (0, 1):
                    total = total + sp[2 * i + x, h, pl.ds(r, 16, stride=2), :]
            sm[4 + i, h, 8:24, :] = 0.25 * total
        return carry

    lax.fori_loop(0, 16, down, 0, unroll=2)
    pack(sm, ysm.at[1], 16)
    h_sm = halo(5, sm, ysm.at[1], yrm.at[1], 16)

    def mid_coeffs(x, carry):
        for h in range(2):
            con = km[x, h, 4:28, :]
            rd = 0.8 / (0.05 + 3.0 * con)
            bm[x, h, 4:28, :] = rd
            gm[x, h, 4:28, :] = rd * con
        return carry

    lax.fori_loop(0, MX, mid_coeffs, 0, unroll=2)
    arrive(h_sm)
    unpack(sm, yrm.at[1], 16, True)

    def mid_first(x, carry):
        for h in range(2):
            v = bm[x, h, 4:28, :] * sm[x, h, 4:28, :]
            bm[x, h, 4:28, :] = v
            m1[x, h, 4:28, :] = v
        return carry

    lax.fori_loop(0, MX, mid_first, 0, unroll=2)
    sweep(m1, m2, gm, bm, 1, 23, 4, 28, 0.25, 2)

    def mid_resid(x, carry):
        v, s = stencil(m2, x, 8, 24, 0.25)
        for h in range(2):
            m1[x, h, 8:24, :] = sm[x, h, 8:24, :] - 0.05 * v[h] - km[x, h, 8:24, :] * (3.0 * v[h] - s[h])
        return carry

    lax.fori_loop(4, 20, mid_resid, 0, unroll=2)

    own_coarse(sc, m1, 4)
    x_sc = coarse_exchange(sc, 1)
    part = jnp.zeros((8, 128), F32)
    for x in range(8):
        for h in range(2):
            part = part + wa[1 + x, h, 16:24, :] * sc[1 + x, h, 16:24, :]
    part = jnp.sum(part, axis=0, keepdims=True)
    message = jnp.where(row == 0, part, jnp.where(row == 1, load, 0.0))
    psend[...] = message
    precv[d] = message
    all_send(psend, precv, ps_sem, pr_sem)
    arrive(x_sc)
    coarse_edges(sc)

    def coarse_first(x, carry):
        for h in range(2):
            v = rc[x, h, 8:32, :] * sc[x, h, 8:32, :]
            rc[x, h, 8:32, :] = v
            ea[x, h, 8:32, :] = v
        return carry

    lax.fori_loop(1, 9, coarse_first, 0)
    for k in range(3):
        sweep(ea, eb, gc, rc, 1, 9, 8, 32, 0.0625, 4)
        sweep(eb, ea, gc, rc, 1, 9, 8, 32, 0.0625, 4)
    sweep(ea, eb, gc, rc, 1, 9, 8, 32, 0.0625, 4)
    all_wait(psend, precv, ps_sem, pr_sem)

    def gather(s, carry):
        return carry + precv[s]

    sums = lax.fori_loop(0, n_dev, gather, jnp.zeros((8, 128), F32), unroll=4)
    sums = jnp.sum(sums, axis=1, keepdims=True)
    shift = jnp.broadcast_to(sums[0:1] / sums[1:2], (8, 128))
    for x in range(8):
        for h in range(2):
            ec[4 + x, h, 8:16, :] = eb[1 + x, h, 16:24, :] + shift
    pack(ec, yse, 8)
    h_ec = halo(6, ec, yse, yre, 8)
    arrive(h_ec)
    unpack(ec, yre, 8, True)

    def mid_up(i, carry):
        for h in range(2):
            v = ec[i, h, 6:18, :]
            for x in (0, 1):
                for r in (0, 1):
                    rows = pl.ds(4 + r, 12, stride=2)
                    m2[2 * i - 4 + x, h, rows, :] = m2[2 * i - 4 + x, h, rows, :] + v
        return carry

    lax.fori_loop(2, 14, mid_up, 0, unroll=2)
    sweep(m2, m1, gm, bm, 2, 22, 4, 28, 0.25, 2)
    sweep(m1, m2, gm, bm, 3, 21, 4, 28, 0.25, 2)

    def fine_up(i, carry):
        for h in range(2):
            v = m2[i, h, 6:26, :]
            for x in (0, 1):
                for r in (0, 1):
                    rows = pl.ds(4 + r, 20, stride=2)
                    p2[2 * i - 4 + x, h, rows, :] = p2[2 * i - 4 + x, h, rows, :] + v
        return carry

    lax.fori_loop(3, 21, fine_up, 0, unroll=2)
    sweep(p2, ca, gg, bb, 3, 37, 4, 44, 1.0, 2)
    sweep(ca, p2, gg, bb, 4, 36, 8, 40, 1.0, 2)
    for h in range(2):
        outs.append(
            pltpu.make_async_copy(
                p2.at[pl.ds(4, 32), h, pl.ds(8, 32), :], pot_out.at[:, :, pl.ds(128 * h, 128)], out_sem.at[4 + h]
            )
        )
        outs[-1].start()
    for copies in (h_conc, h_label, h_phi, h_km, h_flux, h_sm, h_ec, x_kc, x_sc):
        for c in copies:
            c.wait_send()
    for o in outs:
        o.wait()


def body(conc_old, phi_old, solid_pot, phase_label, iface_block, iface_owner):
    n_grp, n_dev = lax.axis_size("grp"), lax.axis_size("dev")
    lists = jnp.concatenate(
        [iface_owner.reshape(2, 128), iface_block.reshape(2, 128), jnp.zeros((4, 128), jnp.int32)], axis=0
    )
    fine = pltpu.VMEM((FX, 2, FY, 128), F32)
    mid = pltpu.VMEM((MX, 2, MY, 128), F32)
    coarse = pltpu.VMEM((GX, 2, GY, 128), F32)
    dma = pltpu.SemaphoreType.DMA
    out = jax.ShapeDtypeStruct(conc_old.shape, F32)
    hbm = pl.BlockSpec(memory_space=pl.ANY)
    return pl.pallas_call(
        functools.partial(kernel, n_grp, n_dev),
        out_shape=(out, out, out),
        in_specs=[hbm, hbm, hbm, hbm, pl.BlockSpec(memory_space=pltpu.VMEM)],
        out_specs=(hbm, hbm, hbm),
        scratch_shapes=[
            fine, pltpu.VMEM((FX, 2, FY, 128), jnp.int32), fine, pltpu.VMEM((32, 2, 32, 128), F32),
            fine, fine, fine, fine, fine, fine, fine, fine, fine, fine,
            mid, mid, mid, mid, mid, mid,
            coarse, coarse, coarse, coarse, coarse, coarse, coarse, coarse, coarse, coarse,
            pltpu.VMEM((EX, 2, EY, 128), F32),
            pltpu.VMEM((3, 2, 16, 2, 8, 128), F32), pltpu.VMEM((3, 2, 20, 2, 8, 128), F32),
            pltpu.VMEM((2, 16, 2, 8, 128), jnp.int32), pltpu.VMEM((2, 20, 2, 8, 128), jnp.int32),
            pltpu.VMEM((2, 2, 8, 2, 8, 128), F32), pltpu.VMEM((2, 2, 12, 2, 8, 128), F32),
            pltpu.VMEM((2, 4, 2, 8, 128), F32), pltpu.VMEM((2, 8, 2, 8, 128), F32),
            pltpu.VMEM((n_dev, 8, 128), jnp.int32), pltpu.VMEM((64, 4096), F32),
            pltpu.VMEM((8, 128), F32), pltpu.VMEM((n_dev, 8, 128), F32),
            dma((8,)), dma((6,)), dma((7, 8)), dma((7, 8)), dma((2, 2)), dma((2, 2)),
            dma((n_dev,)), dma((n_dev,)), dma((n_dev,)), dma((n_dev,)),
        ],
        compiler_params=pltpu.CompilerParams(
            collective_id=0, has_side_effects=True, vmem_limit_bytes=56 * 1024 * 1024
        ),
    )(conc_old, phi_old, solid_pot, phase_label, lists)


def solution(mesh):
    split = P("grp", "dev", None)
    return jax.shard_map(
        body,
        mesh=mesh,
        in_specs=(split, split, split, split, P("grp", "dev"), split),
        out_specs=(split, split, split),
        check_vma=False,
    )
```

```python
import functools

import jax
import jax.numpy as jnp
from jax import lax
from jax.experimental import pallas as pl
from jax.experimental.pallas import tpu as pltpu
from jax.sharding import PartitionSpec as P

MESH = pl.DeviceIdType.MESH
F32 = jnp.float32

FX, FY = 40, 48
MX, MY = 24, 32
EX, EY = 16, 24
GX, GY = 10, 40


def lookup(label, table):
    return jnp.where(label == 0, table[0], jnp.where(label == 1, table[1], table[2])).astype(F32)


def kernel(
    n_grp,
    n_dev,
    conc_hbm,
    phi_hbm,
    solid_hbm,
    label_hbm,
    owner_hbm,
    block_hbm,
    conc_out,
    flux_out,
    pot_out,
    c0, lb, ph, sp, ca, cb, rs, dd, cc, kk, gg, qq, bb, fx, p2,
    sm, km, gm, bm, m1, m2, mu,
    kc, rc, gc, wa, wb, ka, kb, sc, ea, eb,
    ec,
    ysc, yrc, ysl, yrl, ysp, yrp, ysf, yrf, ysu, yru, ysk, yrk, yss, yrs, ysm, yrm, yse, yre,
    lists, lrecv, msk, psend, precv, shifts,
    in_sem, hs_sem, hr_sem, cs_sem, cr_sem, ls_sem, lr_sem, ps_sem, pr_sem, ss_sem, sr_sem,
):
    g = lax.axis_index("grp")
    d = lax.axis_index("dev")
    gu, gd = lax.rem(g + 1, n_grp), lax.rem(g + n_grp - 1, n_grp)
    du, dl = lax.rem(d + 1, n_dev), lax.rem(d + n_dev - 1, n_dev)
    eight = [(gd, dl), (gd, d), (gd, du), (g, dl), (g, du), (gu, dl), (gu, d), (gu, du)]
    lane = lax.broadcasted_iota(jnp.int32, (1, 128), 1)
    l0, l1 = lane == 0, lane == 127

    loads = []
    for k, (src, dst) in enumerate(((conc_hbm, c0), (label_hbm, lb), (phi_hbm, ph))):
        for h in range(2):
            loads.append(
                pltpu.make_async_copy(
                    src.at[:, :, pl.ds(128 * h, 128)], dst.at[pl.ds(4, 32), h, pl.ds(8, 32), :], in_sem.at[2 * k + h]
                )
            )
    for h in range(2):
        loads.append(
            pltpu.make_async_copy(solid_hbm.at[:, :, pl.ds(128 * h, 128)], sp.at[:, h], in_sem.at[6 + h])
        )
    for k, src in enumerate((owner_hbm, block_hbm)):
        loads.append(pltpu.make_async_copy(src, lists.at[k], in_sem.at[8 + k]))
    for load in loads:
        load.start()

    barrier = pltpu.get_barrier_semaphore()
    for t in (eight[0], eight[1], eight[2], eight[5], eight[6], eight[7]):
        pl.semaphore_signal(barrier, inc=1, device_id=t, device_id_type=MESH)

    def greet(j, carry):
        pl.semaphore_signal(barrier, inc=1, device_id=(g, lax.rem(d + j, n_dev)), device_id_type=MESH)
        return carry

    lax.fori_loop(1, n_dev, greet, 0)

    for ref, rows in ((kc, (0, 8, 32, 40)), (sc, (0, 8, 32, 40)), (ka, (0, 8, 32, 40)), (kb, (0, 8, 32, 40)), (ea, (0, 8, 32, 40)), (eb, (0, 8, 32, 40))):
        ref[:, :, 0:8, :] = jnp.zeros((GX, 2, 8, 128), F32)
        ref[:, :, 32:40, :] = jnp.zeros((GX, 2, 8, 128), F32)
        ref[0] = jnp.zeros((2, GY, 128), F32)
        ref[GX - 1] = jnp.zeros((2, GY, 128), F32)

    def pack(field, ys, n, deep):
        def one(x, carry):
            for s, r in ((0, 8), (1, 8 + n - deep)):
                for h in range(2):
                    ys[s, h, pl.ds(deep * x, deep), :] = field[4 + x, h, r : r + deep, :]
            return carry

        lax.fori_loop(0, n, one, 0, unroll=8)

    def unpack(field, yr, n, deep, wide, zero):
        edge_rows = 8 * ((4 * deep + 7) // 8)

        def one(x, carry):
            for s, r, edge in ((0, 8 - deep, d == 0), (1, 8 + n, d == n_dev - 1)):
                for h in range(2):
                    v = yr[s, h, pl.ds(edge_rows + deep * (x - 4), deep), :]
                    field[x, h, r : r + deep, :] = jnp.where(edge, jnp.zeros_like(v), v)
            return carry

        lax.fori_loop(4 - wide, 4 + n + wide, one, 0, unroll=8)
        if zero:
            @pl.when(g == 0)
            def _():
                field[4 - wide : 4] = jnp.zeros(field.at[4 - wide : 4].shape, field.dtype)

            @pl.when(g == n_grp - 1)
            def _():
                field[4 + n : 4 + n + wide] = jnp.zeros(field.at[4 - wide : 4].shape, field.dtype)

    def halo(e, field, ys, yr, n, deep, wide):
        c = 8 * ((4 * deep + 7) // 8)
        m = n * deep
        own = pl.ds(8, n)
        low, high = field.at[pl.ds(4, wide), :, own, :], field.at[pl.ds(4 + n - wide, wide), :, own, :]
        to_low, to_high = field.at[pl.ds(4 - wide, wide), :, own, :], field.at[pl.ds(4 + n, wide), :, own, :]
        first, last, after, before = pl.ds(0, c), pl.ds(m - c, c), pl.ds(c + m, c), pl.ds(0, c)
        pairs = [
            (ys.at[0, :, first], yr.at[1, :, after]),
            (low, to_high),
            (ys.at[1, :, first], yr.at[0, :, after]),
            (ys.at[0], yr.at[1, :, pl.ds(c, m)]),
            (ys.at[1], yr.at[0, :, pl.ds(c, m)]),
            (ys.at[0, :, last], yr.at[1, :, before]),
            (high, to_low),
            (ys.at[1, :, last], yr.at[0, :, before]),
        ]
        copies = []
        for i in (0, 2, 5, 7, 4, 3, 6, 1):
            src, dst = pairs[i]
            copies.append(
                pltpu.make_async_remote_copy(
                    src_ref=src, dst_ref=dst, send_sem=hs_sem.at[e, i], recv_sem=hr_sem.at[e, i],
                    device_id=eight[i], device_id_type=MESH,
                )
            )
        for c in copies:
            c.start()
        return copies

    def sent(copies):
        for c in copies:
            c.wait_send()

    def arrive(copies):
        for c in copies:
            c.wait_recv()

    def all_send(src, dst, send_sem, recv_sem):
        def one(j, carry):
            pltpu.make_async_remote_copy(
                src_ref=src, dst_ref=dst.at[d], send_sem=send_sem.at[j], recv_sem=recv_sem.at[d],
                device_id=(g, lax.rem(d + j, n_dev)), device_id_type=MESH,
            ).start()
            return carry

        lax.fori_loop(1, n_dev, one, 0)

    def all_wait(src, dst, send_sem, recv_sem):
        def one(j, carry):
            s = lax.rem(d + n_dev - j, n_dev)
            c = pltpu.make_async_remote_copy(
                src_ref=src, dst_ref=dst.at[s], send_sem=send_sem.at[j], recv_sem=recv_sem.at[s],
                device_id=(g, lax.rem(d + j, n_dev)), device_id_type=MESH,
            )
            c.wait_recv()
            c.wait_send()
            return carry

        lax.fori_loop(1, n_dev, one, 0)

    def z_sum(a, b):
        ra, rb = pltpu.roll(a, 1, 1), pltpu.roll(b, 1, 1)
        sa, sb = pltpu.roll(a, 127, 1), pltpu.roll(b, 127, 1)
        zero = jnp.zeros_like(a)
        za = jnp.where(l0, zero, ra) + jnp.where(l1, sb, sa)
        zb = jnp.where(l0, ra, rb) + jnp.where(l1, zero, sb)
        return za, zb

    def plane(field, x, h, r0, r1):
        return (field[x - 1, h, r0:r1, :] + field[x + 1, h, r0:r1, :]) + (
            field[x, h, r0 - 1 : r1 - 1, :] + field[x, h, r0 + 1 : r1 + 1, :]
        )

    def stencil(field, x, r0, r1, weight):
        a, b = field[x, 0, r0:r1, :], field[x, 1, r0:r1, :]
        za, zb = z_sum(a, b)
        pa, pb = plane(field, x, 0, r0, r1), plane(field, x, 1, r0, r1)
        if weight != 1.0:
            pa, pb = weight * pa, weight * pb
        return (a, b), (pa + za, pb + zb)

    def sweep(src, dst, gain, rhs, x0, x1, r0, r1, weight, unroll):
        def one(x, carry):
            v, s = stencil(src, x, r0, r1, weight)
            for h in range(2):
                dst[x, h, r0:r1, :] = 0.2 * v[h] + rhs[x, h, r0:r1, :] + gain[x, h, r0:r1, :] * s[h]
            return carry

        lax.fori_loop(x0, x1, one, 0, unroll=unroll)

    for k in range(4):
        loads[k].wait()
    pack(c0, ysc, 32, 4)
    pack(lb, ysl, 32, 3)

    def conc_coeffs(x, r0, r1):
        for h in range(2):
            old = c0[x, h, r0:r1, :]
            label = lb[x, h, r0:r1, :]
            dd[x, h, r0:r1, :] = jnp.where(old > 0.0, lookup(label, (1.5 / 10.0, 0.1 / 1.6, 0.4 / 3.4)), 0.0)
            cc[x, h, r0:r1, :] = old * lookup(label, (1.0 / 10.0, 1.0 / 1.6, 1.0 / 3.4))

    def pot_coeffs(x, r0, r1):
        for h in range(2):
            con = lookup(lb[x, h, r0:r1, :], (1.0, 0.3, 0.6)) * c0[x, h, r0:r1, :]
            rd = 0.8 / (0.05 + 6.0 * con)
            kk[x, h, r0:r1, :] = con
            bb[x, h, r0:r1, :] = rd
            gg[x, h, r0:r1, :] = rd * con

    def each(lo, hi, unroll, *fns):
        def one(x, carry):
            for fn in fns:
                fn(x)
            return carry

        lax.fori_loop(lo, hi, one, 0, unroll=unroll)

    each(4, 36, 4, lambda x: conc_coeffs(x, 8, 40), lambda x: pot_coeffs(x, 8, 40))
    loads[4].wait()
    loads[5].wait()
    pack(ph, ysp, 32, 3)
    loads[8].wait()
    loads[9].wait()
    lrecv[d] = lists[...]

    def own_mid(i, carry):
        for h in range(2):
            total = jnp.zeros((16, 128), F32)
            for x in (0, 1):
                for r in (0, 1):
                    rows = pl.ds(8 + r, 16, stride=2)
                    total = total + kk[4 + 2 * i + x, h, rows, :]
            km[4 + i, h, 8:24, :] = 0.25 * total
        return carry

    lax.fori_loop(0, 16, own_mid, 0, unroll=4)
    pack(km, ysk, 16, 2)

    def own_coarse(dst, src, off):
        def one(i, carry):
            for h in range(2):
                total = jnp.zeros((8, 128), F32)
                for x in (0, 1):
                    for r in (0, 1):
                        total = total + src[off + 2 * i + x, h, pl.ds(8 + r, 8, stride=2), :]
                dst[1 + i, h, 16:24, :] = 0.25 * total
            return carry

        lax.fori_loop(0, 8, one, 0, unroll=8)

    def coarse_exchange(field, k):
        copies = []
        for i, (t, r) in enumerate((((g, dl), 24), ((g, du), 8))):
            copies.append(
                pltpu.make_async_remote_copy(
                    src_ref=field.at[pl.ds(1, 8), :, pl.ds(16, 8), :], dst_ref=field.at[pl.ds(1, 8), :, pl.ds(r, 8), :],
                    send_sem=cs_sem.at[k, i], recv_sem=cr_sem.at[k, i], device_id=t, device_id_type=MESH,
                )
            )
        for c in copies:
            c.start()
        return copies

    def coarse_edges(field):
        @pl.when(d == 0)
        def _():
            field[:, :, 8:16, :] = jnp.zeros((GX, 2, 8, 128), F32)

        @pl.when(d == n_dev - 1)
        def _():
            field[:, :, 24:32, :] = jnp.zeros((GX, 2, 8, 128), F32)

    own_coarse(kc, km, 4)

    pl.semaphore_wait(barrier, n_dev - 1 + 6)
    h_conc = halo(0, c0, ysc, yrc, 32, 4, 4)
    h_label = halo(1, lb, ysl, yrl, 32, 3, 3)
    all_send(lists, lrecv, ls_sem, lr_sem)
    for k in (6, 7):
        loads[k].wait()
    all_wait(lists, lrecv, ls_sem, lr_sem)

    def count(s, carry):
        total = carry
        for r in range(2):
            owner, block = lrecv[s, 0, r : r + 1, :], lrecv[s, 1, r : r + 1, :]
            place = jnp.where(owner == d, (block & 1) * 32 + ((block >> 1) & 31), -1)
            column = block >> 6
            rows = (lax.broadcasted_iota(jnp.int32, (64, 128), 0) == place).astype(jnp.bfloat16)
            cols = (lax.broadcasted_iota(jnp.int32, (32, 128), 0) == column).astype(jnp.bfloat16)
            total = total + lax.dot_general(
                rows, cols, (((1,), (1,)), ((), ())), preferred_element_type=F32
            )
        return total

    counts = lax.fori_loop(0, n_dev, count, jnp.zeros((64, 32), F32), unroll=8)
    named = jnp.where(counts > 0.0, 1.0, 0.0).astype(jnp.bfloat16)
    spread = (
        lax.broadcasted_iota(jnp.int32, (32, 4096), 1) // 128 == lax.broadcasted_iota(jnp.int32, (32, 4096), 0)
    ).astype(jnp.bfloat16)
    msk[...] = jnp.dot(named, spread, preferred_element_type=F32)
    arrive(h_conc)
    unpack(c0, yrc, 32, 4, 4, True)
    arrive(h_label)
    unpack(lb, yrl, 32, 3, 3, False)
    h_phi = halo(2, ph, ysp, yrp, 32, 3, 3)
    x_kc = coarse_exchange(kc, 0)
    each(1, 4, 3, lambda x: conc_coeffs(x, 0, 48))
    each(36, 39, 3, lambda x: conc_coeffs(x, 0, 48))
    each(4, 36, 8, lambda x: conc_coeffs(x, 0, 8), lambda x: conc_coeffs(x, 40, 48))

    def conc_sweep(src, dst, x0, x1, r0, r1, unroll):
        def one(x, carry):
            _, s = stencil(src, x, r0, r1, 1.0)
            for h in range(2):
                v = cc[x, h, r0:r1, :] + dd[x, h, r0:r1, :] * s[h]
                if dst is None:
                    conc_out[x - 4, :, 128 * h : 128 * h + 128] = v
                else:
                    dst[x, h, r0:r1, :] = v
            return carry

        lax.fori_loop(x0, x1, one, 0, unroll=unroll)

    conc_sweep(c0, ca, 1, 39, 4, 44, 19)
    conc_sweep(ca, cb, 2, 38, 4, 44, 18)
    conc_sweep(cb, ca, 3, 37, 4, 44, 17)
    conc_sweep(ca, None, 4, 36, 8, 40, 16)

    for x in range(32):
        for h in range(2):
            con = conc_out[x, :, 128 * h : 128 * h + 128]
            u = 0.5 * (sp[x, h] - ph[4 + x, h, 8:40, :]) - 0.1 * jnp.log(con)
            kin = lookup(lb[4 + x, h, 8:40, :], (0.2, 1.0, 0.5)) * jnp.sqrt(con)
            val = kin * (jnp.exp(u) - jnp.exp(-u))
            val = msk[32 * h : 32 * h + 32, 128 * x : 128 * x + 128] * val
            fx[4 + x, h, 8:40, :] = val
            flux_out[x, :, 128 * h : 128 * h + 128] = val
    pack(fx, ysf, 32, 2)
    h_flux = halo(4, fx, ysf, yrf, 32, 2, 2)

    each(2, 4, 2, lambda x: pot_coeffs(x, 0, 48))
    each(36, 38, 2, lambda x: pot_coeffs(x, 0, 48))
    each(4, 36, 8, lambda x: pot_coeffs(x, 0, 8), lambda x: pot_coeffs(x, 40, 48))
    arrive(h_phi)
    unpack(ph, yrp, 32, 3, 3, True)

    def first(x, carry):
        v, s = stencil(ph, x, 4, 44, 1.0)
        for h in range(2):
            rd = bb[x, h, 4:44, :]
            qq[x, h, 4:44, :] = (0.2 + 0.05 * rd) * v[h] + gg[x, h, 4:44, :] * s[h]
        return carry

    lax.fori_loop(2, 38, first, 0, unroll=12)
    arrive(x_kc)
    coarse_edges(kc)

    def coarse_coeffs(x, carry):
        for h in range(2):
            con = kc[x, h, 8:32, :]
            rd = 0.8 / (0.05 + 2.25 * con)
            rc[x, h, 8:32, :] = rd
            gc[x, h, 8:32, :] = rd * con
            wa[x, h, 8:32, :] = jnp.ones((24, 128), F32)
            ka[x, h, 8:32, :] = con
        return carry

    lax.fori_loop(1, 9, coarse_coeffs, 0, unroll=4)

    def dual(w_in, k_in, w_out, k_out):
        def one(x, carry):
            v, s = stencil(k_in, x, 8, 32, 0.0625)
            for h in range(2):
                w = w_in[x, h, 8:32, :]
                w = w - rc[x, h, 8:32, :] * (0.05 * w + 2.25 * v[h] - s[h])
                w_out[x, h, 8:32, :] = w
                k_out[x, h, 8:32, :] = kc[x, h, 8:32, :] * w
            return carry

        lax.fori_loop(1, 9, one, 0, unroll=8)

    for k in range(4):
        dual(wa, ka, wb, kb)
        dual(wb, kb, wa, ka)

    load = jnp.zeros((8, 128), F32)
    row = lax.broadcasted_iota(jnp.int32, (8, 128), 0)
    lane8 = lax.broadcasted_iota(jnp.int32, (8, 128), 1)
    edge_y = jnp.where(((row == 0) & (d == 0)) | ((row == 7) & (d == n_dev - 1)), 1.0, 0.0)
    for x in range(8):
        for h in range(2):
            edge_z = jnp.where(lane8 == 127 * h, 1.0, 0.0)
            edge_xy = edge_y + (1.0 if x in (0, 7) else 0.0)
            load = load + (0.05 + kc[1 + x, h, 16:24, :] * (0.0625 * edge_xy + edge_z))
    load = jnp.sum(load, axis=0, keepdims=True)
    row2 = lax.broadcasted_iota(jnp.int32, (2, 128), 0)

    arrive(h_flux)
    unpack(fx, yrf, 32, 2, 2, True)
    h_km = halo(3, km, ysk, yrk, 16, 2, 2)

    def second(x, carry):
        for h in range(2):
            rd = bb[x, h, 4:44, :]
            fl = fx[x, h, 4:44, :]
            ca[x, h, 4:44, :] = qq[x, h, 4:44, :] + rd * fl
            src = 0.05 * ph[x, h, 4:44, :] + fl
            qq[x, h, 4:44, :] = src
            bb[x, h, 4:44, :] = rd * src
        return carry

    lax.fori_loop(2, 38, second, 0, unroll=6)
    sweep(ca, p2, gg, bb, 3, 37, 4, 44, 1.0, 17)

    def resid(x, carry):
        v, s = stencil(p2, x, 8, 40, 1.0)
        for h in range(2):
            rs[x - 4, h] = qq[x, h, 8:40, :] - 0.05 * v[h] - kk[x, h, 8:40, :] * (6.0 * v[h] - s[h])
        return carry

    lax.fori_loop(4, 36, resid, 0, unroll=16)

    def down(i, carry):
        for h in range(2):
            total = jnp.zeros((16, 128), F32)
            for x in (0, 1):
                for r in (0, 1):
                    total = total + rs[2 * i + x, h, pl.ds(r, 16, stride=2), :]
            sm[4 + i, h, 8:24, :] = 0.25 * total
        return carry

    lax.fori_loop(0, 16, down, 0, unroll=8)
    pack(sm, yss, 16, 2)
    h_sm = halo(5, sm, yss, yrs, 16, 2, 2)
    pack(p2, ysu, 32, 2)
    arrive(h_km)
    unpack(km, yrk, 16, 2, 2, True)

    def mid_coeffs(x, carry):
        for h in range(2):
            con = km[x, h, 4:28, :]
            rd = 0.8 / (0.05 + 3.0 * con)
            bm[x, h, 4:28, :] = rd
            gm[x, h, 4:28, :] = rd * con
        return carry

    lax.fori_loop(2, 22, mid_coeffs, 0, unroll=5)
    arrive(h_sm)
    unpack(sm, yrs, 16, 2, 2, True)
    h_p2 = halo(7, p2, ysu, yru, 32, 2, 2)

    def mid_first(x, carry):
        for h in range(2):
            v = bm[x, h, 4:28, :] * sm[x, h, 4:28, :]
            bm[x, h, 4:28, :] = v
            m1[x, h, 4:28, :] = v
        return carry

    lax.fori_loop(2, 22, mid_first, 0, unroll=10)
    sweep(m1, m2, gm, bm, 3, 21, 4, 28, 0.25, 18)

    def mid_resid(x, carry):
        v, s = stencil(m2, x, 8, 24, 0.25)
        for h in range(2):
            m1[x, h, 8:24, :] = sm[x, h, 8:24, :] - 0.05 * v[h] - km[x, h, 8:24, :] * (3.0 * v[h] - s[h])
            mu[x, h, 8:24, :] = v[h]
        return carry

    lax.fori_loop(4, 20, mid_resid, 0, unroll=16)

    own_coarse(sc, m1, 4)
    x_sc = coarse_exchange(sc, 1)
    part = jnp.zeros((8, 128), F32)
    for x in range(8):
        for h in range(2):
            part = part + wa[1 + x, h, 16:24, :] * sc[1 + x, h, 16:24, :]
    part = jnp.sum(part, axis=0, keepdims=True)
    message = jnp.where(row2 == 0, jnp.broadcast_to(part, (2, 128)), jnp.broadcast_to(load, (2, 128)))
    psend[...] = message
    precv[d] = message
    all_send(psend, precv, ps_sem, pr_sem)
    pack(mu, ysm, 16, 3)
    h_mu = halo(8, mu, ysm, yrm, 16, 3, 3)
    arrive(x_sc)
    coarse_edges(sc)

    def coarse_first(x, carry):
        for h in range(2):
            v = rc[x, h, 8:32, :] * sc[x, h, 8:32, :]
            rc[x, h, 8:32, :] = v
            ea[x, h, 8:32, :] = v
        return carry

    lax.fori_loop(1, 9, coarse_first, 0, unroll=8)
    for k in range(3):
        sweep(ea, eb, gc, rc, 1, 9, 8, 32, 0.0625, 8)
        sweep(eb, ea, gc, rc, 1, 9, 8, 32, 0.0625, 8)
    sweep(ea, eb, gc, rc, 1, 9, 8, 32, 0.0625, 8)
    for x in range(8):
        for h in range(2):
            ec[4 + x, h, 8:16, :] = eb[1 + x, h, 16:24, :]
    pack(ec, yse, 8, 2)
    h_ec = halo(6, ec, yse, yre, 8, 2, 2)
    all_wait(psend, precv, ps_sem, pr_sem)

    def gather(s, carry):
        return carry + precv[s]

    sums = lax.fori_loop(0, n_dev, gather, jnp.zeros((2, 128), F32), unroll=8)
    sums = jnp.sum(sums, axis=1, keepdims=True)
    shifts[1] = jnp.broadcast_to(sums[0:1] / sums[1:2], (8, 128))
    x_shift = []
    for k, (t, i) in enumerate((((gd, d), 2), ((gu, d), 0))):
        x_shift.append(
            pltpu.make_async_remote_copy(
                src_ref=shifts.at[1], dst_ref=shifts.at[i], send_sem=ss_sem.at[k], recv_sem=sr_sem.at[k],
                device_id=t, device_id_type=MESH,
            )
        )
    for c in x_shift:
        c.start()
    arrive(h_mu)
    sent(h_mu)
    unpack(mu, yrm, 16, 3, 3, True)
    arrive(h_p2)
    sent(h_p2)
    unpack(p2, yru, 32, 2, 2, True)
    arrive(h_ec)
    unpack(ec, yre, 8, 2, 2, True)
    arrive(x_shift)

    row12 = lax.broadcasted_iota(jnp.int32, (12, 128), 0)
    inside = jnp.where(((row12 < 2) & (d == 0)) | ((row12 >= 10) & (d == n_dev - 1)), 0.0, 1.0)
    own_shift = inside * shifts[1, 0:1, :]
    low_shift = jnp.where(g == 0, jnp.zeros((12, 128), F32), inside * shifts[0, 0:1, :])
    high_shift = jnp.where(g == n_grp - 1, jnp.zeros((12, 128), F32), inside * shifts[2, 0:1, :])
    for i in range(2, 14):
        for h in range(2):
            v = ec[i, h, 6:18, :] + (low_shift if i < 4 else own_shift if i < 12 else high_shift)
            for x in (0, 1):
                if not 1 <= 2 * i - 4 + x < 23:
                    continue
                for r in (0, 1):
                    rows = pl.ds(4 + r, 12, stride=2)
                    mu[2 * i - 4 + x, h, rows, :] = mu[2 * i - 4 + x, h, rows, :] + v
    sweep(mu, m1, gm, bm, 2, 22, 4, 28, 0.25, 10)
    sweep(m1, m2, gm, bm, 3, 21, 4, 28, 0.25, 18)

    def fine_up(i, carry):
        for h in range(2):
            v = m2[i, h, 6:26, :]
            for x in (0, 1):
                for r in (0, 1):
                    rows = pl.ds(4 + r, 20, stride=2)
                    p2[2 * i - 4 + x, h, rows, :] = p2[2 * i - 4 + x, h, rows, :] + v
        return carry

    lax.fori_loop(3, 21, fine_up, 0, unroll=6)
    sweep(p2, ca, gg, bb, 3, 37, 4, 44, 1.0, 17)

    def last(x, carry):
        v, s = stencil(ca, x, 8, 40, 1.0)
        for h in range(2):
            new = 0.2 * v[h] + bb[x, h, 8:40, :] + gg[x, h, 8:40, :] * s[h]
            pot_out[x - 4, :, 128 * h : 128 * h + 128] = new
        return carry

    lax.fori_loop(4, 36, last, 0, unroll=16)
    for copies in (h_conc, h_label, h_phi, h_km, h_flux, h_sm, h_ec, x_kc, x_sc, x_shift):
        sent(copies)


def store(conc, flux, pot, conc_out, flux_out, pot_out, sem):
    copies = [
        pltpu.make_async_copy(src, dst, sem.at[k])
        for k, (src, dst) in enumerate(((conc, conc_out), (flux, flux_out), (pot, pot_out)))
    ]
    for c in copies:
        c.start()
    for c in copies:
        c.wait()


def body(conc_old, phi_old, solid_pot, phase_label, iface_block, iface_owner):
    n_grp, n_dev = lax.axis_size("grp"), lax.axis_size("dev")
    fine = pltpu.VMEM((FX, 2, FY, 128), F32)
    mid = pltpu.VMEM((MX, 2, MY, 128), F32)
    coarse = pltpu.VMEM((GX, 2, GY, 128), F32)
    dma = pltpu.SemaphoreType.DMA
    out = jax.ShapeDtypeStruct(conc_old.shape, F32)
    kept = pltpu.VMEM(conc_old.shape, F32)
    hbm = pl.BlockSpec(memory_space=pl.ANY)
    vmem = pl.BlockSpec(memory_space=pltpu.VMEM)

    def faces(n, deep, dtype=F32):
        c = 8 * ((4 * deep + 7) // 8)
        return [pltpu.VMEM((2, 2, n * deep, 128), dtype), pltpu.VMEM((2, 2, n * deep + 2 * c, 128), dtype)]

    fields = pl.pallas_call(
        functools.partial(kernel, n_grp, n_dev),
        out_shape=(kept, kept, kept),
        in_specs=[hbm] * 6,
        out_specs=(vmem, vmem, vmem),
        scratch_shapes=[
            fine, pltpu.VMEM((FX, 2, FY, 128), jnp.int32), fine, pltpu.VMEM((32, 2, 32, 128), F32),
            fine, fine, pltpu.VMEM((32, 2, 32, 128), F32), fine, fine, fine, fine, fine, fine, fine, fine,
            mid, mid, mid, mid, mid, mid, mid,
            coarse, coarse, coarse, coarse, coarse, coarse, coarse, coarse, coarse, coarse,
            pltpu.VMEM((EX, 2, EY, 128), F32),
            *faces(32, 4), *faces(32, 3, jnp.int32), *faces(32, 3), *faces(32, 2), *faces(32, 2),
            *faces(16, 2), *faces(16, 2), *faces(16, 3), *faces(8, 2),
            pltpu.VMEM((2, 2, 128), jnp.int32), pltpu.VMEM((n_dev, 2, 2, 128), jnp.int32), pltpu.VMEM((64, 4096), F32),
            pltpu.VMEM((2, 128), F32), pltpu.VMEM((n_dev, 2, 128), F32), pltpu.VMEM((3, 8, 128), F32),
            dma((10,)), dma((9, 8)), dma((9, 8)), dma((2, 2)), dma((2, 2)),
            dma((n_dev,)), dma((n_dev,)), dma((n_dev,)), dma((n_dev,)), dma((2,)), dma((2,)),
        ],
        compiler_params=pltpu.CompilerParams(
            collective_id=0, has_side_effects=True, vmem_limit_bytes=50 * 1024 * 1024
        ),
    )(conc_old, phi_old, solid_pot, phase_label, iface_owner.reshape(2, 128), iface_block.reshape(2, 128))
    return pl.pallas_call(
        store,
        out_shape=(out, out, out),
        in_specs=[vmem] * 3,
        out_specs=(hbm, hbm, hbm),
        scratch_shapes=[dma((3,))],
    )(*[pltpu.with_memory_space_constraint(field, pltpu.VMEM) for field in fields])


def solution(mesh):
    split = P("grp", "dev", None)
    return jax.shard_map(
        body,
        mesh=mesh,
        in_specs=(split, split, split, split, P("grp", "dev"), split),
        out_specs=(split, split, split),
        check_vma=False,
    )
```

```python
import functools

import jax
import jax.numpy as jnp
from jax import lax
from jax.experimental import pallas as pl
from jax.experimental.pallas import tpu as pltpu
from jax.sharding import PartitionSpec as P

MESH = pl.DeviceIdType.MESH
F32 = jnp.float32

FX, FY = 40, 48
MX, MY = 24, 32
EX, EY = 16, 24
GX, GY = 10, 40


def lookup(label, table):
    return jnp.where(label == 0, table[0], jnp.where(label == 1, table[1], table[2])).astype(F32)


def z_sum(a, b):
    lane = lax.broadcasted_iota(jnp.int32, (1, 128), 1)
    l0, l1 = lane == 0, lane == 127
    ra, rb = pltpu.roll(a, 1, 1), pltpu.roll(b, 1, 1)
    sa, sb = pltpu.roll(a, 127, 1), pltpu.roll(b, 127, 1)
    zero = jnp.zeros_like(a)
    za = jnp.where(l0, zero, ra) + jnp.where(l1, sb, sa)
    zb = jnp.where(l0, ra, rb) + jnp.where(l1, zero, sb)
    return za, zb


def plane(field, x, h, r0, r1):
    return (field[x - 1, h, r0:r1, :] + field[x + 1, h, r0:r1, :]) + (
        field[x, h, r0 - 1 : r1 - 1, :] + field[x, h, r0 + 1 : r1 + 1, :]
    )


def stencil(field, x, r0, r1, weight):
    a, b = field[x, 0, r0:r1, :], field[x, 1, r0:r1, :]
    za, zb = z_sum(a, b)
    pa, pb = plane(field, x, 0, r0, r1), plane(field, x, 1, r0, r1)
    if weight != 1.0:
        pa, pb = weight * pa, weight * pb
    return (a, b), (pa + za, pb + zb)


def kernel(
    n_grp,
    n_dev,
    conc_hbm,
    phi_hbm,
    solid_hbm,
    label_hbm,
    owner_hbm,
    block_hbm,
    conc_out,
    flux_out,
    ca,
    gg,
    bb,
    c0, lb, ph, sp, cb, cd, rs, dd, cc, kk, qq, fx, p2,
    sm, km, gm, bm, m1, m2, mu,
    kc, rc, gc, wa, wb, ka, kb, sc, ea, eb,
    ec,
    ysc, yrc, ysl, yrl, ysp, yrp, ysf, yrf, ysu, yru, ysk, yrk, yss, yrs, ysm, yrm, yse, yre,
    lists, lrecv, msk, psend, precv, shifts,
    in_sem, hs_sem, hr_sem, cs_sem, cr_sem, ls_sem, lr_sem, ps_sem, pr_sem, ss_sem, sr_sem,
):
    g = lax.axis_index("grp")
    d = lax.axis_index("dev")
    gu, gd = lax.rem(g + 1, n_grp), lax.rem(g + n_grp - 1, n_grp)
    du, dl = lax.rem(d + 1, n_dev), lax.rem(d + n_dev - 1, n_dev)
    eight = [(gd, dl), (gd, d), (gd, du), (g, dl), (g, du), (gu, dl), (gu, d), (gu, du)]

    loads = []
    for k, (src, dst) in enumerate(((conc_hbm, c0), (label_hbm, lb), (phi_hbm, ph))):
        for h in range(2):
            loads.append(
                pltpu.make_async_copy(
                    src.at[:, :, pl.ds(128 * h, 128)], dst.at[pl.ds(4, 32), h, pl.ds(8, 32), :], in_sem.at[2 * k + h]
                )
            )
    for h in range(2):
        loads.append(
            pltpu.make_async_copy(solid_hbm.at[:, :, pl.ds(128 * h, 128)], sp.at[:, h], in_sem.at[6 + h])
        )
    for k, src in enumerate((owner_hbm, block_hbm)):
        for r in range(2):
            loads.append(
                pltpu.make_async_copy(src.at[:, pl.ds(128 * r, 128)], lists.at[k, r], in_sem.at[8 + 2 * k + r])
            )
    for load in loads:
        load.start()

    barrier = pltpu.get_barrier_semaphore()
    for t in (eight[0], eight[1], eight[2], eight[5], eight[6], eight[7]):
        pl.semaphore_signal(barrier, inc=1, device_id=t, device_id_type=MESH)

    def greet(j, carry):
        pl.semaphore_signal(barrier, inc=1, device_id=(g, lax.rem(d + j, n_dev)), device_id_type=MESH)
        return carry

    lax.fori_loop(1, n_dev, greet, 0)

    for ref, rows in ((kc, (0, 8, 32, 40)), (sc, (0, 8, 32, 40)), (ka, (0, 8, 32, 40)), (kb, (0, 8, 32, 40)), (ea, (0, 8, 32, 40)), (eb, (0, 8, 32, 40))):
        ref[:, :, 0:8, :] = jnp.zeros((GX, 2, 8, 128), F32)
        ref[:, :, 32:40, :] = jnp.zeros((GX, 2, 8, 128), F32)
        ref[0] = jnp.zeros((2, GY, 128), F32)
        ref[GX - 1] = jnp.zeros((2, GY, 128), F32)

    def pack(field, ys, n, deep, off=0):
        def one(x, carry):
            for s, r in ((0, 8 + off), (1, 8 + n - deep - off)):
                for h in range(2):
                    ys[s, h, pl.ds(deep * x, deep), :] = field[4 + x, h, r : r + deep, :]
            return carry

        lax.fori_loop(0, n, one, 0, unroll=8)

    def unpack(field, yr, n, deep, wide, zero, off=0, corners=True):
        edge_rows = 8 * ((4 * deep + 7) // 8)

        def one(x, carry):
            for s, r, edge in ((0, 8 - deep - off, d == 0), (1, 8 + n + off, d == n_dev - 1)):
                for h in range(2):
                    v = yr[s, h, pl.ds(edge_rows + deep * (x - 4), deep), :]
                    field[x, h, r : r + deep, :] = jnp.where(edge, jnp.zeros_like(v), v)
            return carry

        reach = wide if corners else 0
        lax.fori_loop(4 - reach, 4 + n + reach, one, 0, unroll=8)
        if zero:
            @pl.when(g == 0)
            def _():
                field[4 - wide - off : 4 - off] = jnp.zeros(field.at[4 - wide : 4].shape, field.dtype)

            @pl.when(g == n_grp - 1)
            def _():
                field[4 + n + off : 4 + n + wide + off] = jnp.zeros(field.at[4 - wide : 4].shape, field.dtype)

    def halo(e, field, ys, yr, n, deep, wide, off=0, corners=True):
        c = 8 * ((4 * deep + 7) // 8)
        m = n * deep
        own = pl.ds(8, n)
        low, high = field.at[pl.ds(4 + off, wide), :, own, :], field.at[pl.ds(4 + n - wide - off, wide), :, own, :]
        to_low, to_high = field.at[pl.ds(4 - wide - off, wide), :, own, :], field.at[pl.ds(4 + n + off, wide), :, own, :]
        first, last, after, before = pl.ds(0, c), pl.ds(m - c, c), pl.ds(c + m, c), pl.ds(0, c)
        pairs = [
            (ys.at[0, :, first], yr.at[1, :, after]),
            (low, to_high),
            (ys.at[1, :, first], yr.at[0, :, after]),
            (ys.at[0], yr.at[1, :, pl.ds(c, m)]),
            (ys.at[1], yr.at[0, :, pl.ds(c, m)]),
            (ys.at[0, :, last], yr.at[1, :, before]),
            (high, to_low),
            (ys.at[1, :, last], yr.at[0, :, before]),
        ]
        copies = []
        for i in (0, 2, 5, 7, 4, 3, 6, 1) if corners else (4, 3, 6, 1):
            src, dst = pairs[i]
            copies.append(
                pltpu.make_async_remote_copy(
                    src_ref=src, dst_ref=dst, send_sem=hs_sem.at[e, i], recv_sem=hr_sem.at[e, i],
                    device_id=eight[i], device_id_type=MESH,
                )
            )
        for c in copies:
            c.start()
        return copies

    def sent(copies):
        for c in copies:
            c.wait_send()

    def arrive(copies):
        for c in copies:
            c.wait_recv()

    def all_send(src, dst, send_sem, recv_sem):
        def one(j, carry):
            pltpu.make_async_remote_copy(
                src_ref=src, dst_ref=dst.at[d], send_sem=send_sem.at[j], recv_sem=recv_sem.at[d],
                device_id=(g, lax.rem(d + j, n_dev)), device_id_type=MESH,
            ).start()
            return carry

        lax.fori_loop(1, n_dev, one, 0)

    def all_wait(src, dst, send_sem, recv_sem):
        def one(j, carry):
            s = lax.rem(d + n_dev - j, n_dev)
            c = pltpu.make_async_remote_copy(
                src_ref=src, dst_ref=dst.at[s], send_sem=send_sem.at[j], recv_sem=recv_sem.at[s],
                device_id=(g, lax.rem(d + j, n_dev)), device_id_type=MESH,
            )
            c.wait_recv()
            c.wait_send()
            return carry

        lax.fori_loop(1, n_dev, one, 0)

    def sweep(src, dst, gain, rhs, x0, x1, r0, r1, weight, unroll):
        def one(x, carry):
            v, s = stencil(src, x, r0, r1, weight)
            for h in range(2):
                dst[x, h, r0:r1, :] = 0.2 * v[h] + rhs[x, h, r0:r1, :] + gain[x, h, r0:r1, :] * s[h]
            return carry

        lax.fori_loop(x0, x1, one, 0, unroll=unroll)

    for k in range(4):
        loads[k].wait()
    pack(c0, ysc, 32, 4)
    pack(lb, ysl, 32, 3)

    def conc_coeffs(x, r0, r1):
        for h in range(2):
            old = c0[x, h, r0:r1, :]
            label = lb[x, h, r0:r1, :]
            dd[x, h, r0:r1, :] = jnp.where(old > 0.0, lookup(label, (1.5 / 10.0, 0.1 / 1.6, 0.4 / 3.4)), 0.0)
            cc[x, h, r0:r1, :] = old * lookup(label, (1.0 / 10.0, 1.0 / 1.6, 1.0 / 3.4))

    def pot_coeffs(x, r0, r1):
        for h in range(2):
            con = lookup(lb[x, h, r0:r1, :], (1.0, 0.3, 0.6)) * c0[x, h, r0:r1, :]
            rd = 0.8 / (0.05 + 6.0 * con)
            kk[x, h, r0:r1, :] = con
            bb[x, h, r0:r1, :] = rd
            gg[x, h, r0:r1, :] = rd * con

    def each(lo, hi, unroll, *fns):
        def one(x, carry):
            for fn in fns:
                fn(x)
            return carry

        lax.fori_loop(lo, hi, one, 0, unroll=unroll)

    each(4, 36, 4, lambda x: conc_coeffs(x, 8, 40), lambda x: pot_coeffs(x, 8, 40))
    loads[4].wait()
    loads[5].wait()
    pack(ph, ysp, 32, 3)
    for k in range(8, 12):
        loads[k].wait()
    lrecv[d] = lists[...]

    def own_mid(i, carry):
        for h in range(2):
            total = jnp.zeros((16, 128), F32)
            for x in (0, 1):
                for r in (0, 1):
                    rows = pl.ds(8 + r, 16, stride=2)
                    total = total + kk[4 + 2 * i + x, h, rows, :]
            km[4 + i, h, 8:24, :] = 0.25 * total
        return carry

    lax.fori_loop(0, 16, own_mid, 0, unroll=4)
    pack(km, ysk, 16, 2)

    def own_coarse(dst, src, off):
        def one(i, carry):
            for h in range(2):
                total = jnp.zeros((8, 128), F32)
                for x in (0, 1):
                    for r in (0, 1):
                        total = total + src[off + 2 * i + x, h, pl.ds(8 + r, 8, stride=2), :]
                dst[1 + i, h, 16:24, :] = 0.25 * total
            return carry

        lax.fori_loop(0, 8, one, 0, unroll=8)

    def coarse_exchange(field, k):
        copies = []
        for i, (t, r) in enumerate((((g, dl), 24), ((g, du), 8))):
            copies.append(
                pltpu.make_async_remote_copy(
                    src_ref=field.at[pl.ds(1, 8), :, pl.ds(16, 8), :], dst_ref=field.at[pl.ds(1, 8), :, pl.ds(r, 8), :],
                    send_sem=cs_sem.at[k, i], recv_sem=cr_sem.at[k, i], device_id=t, device_id_type=MESH,
                )
            )
        for c in copies:
            c.start()
        return copies

    def coarse_edges(field):
        @pl.when(d == 0)
        def _():
            field[:, :, 8:16, :] = jnp.zeros((GX, 2, 8, 128), F32)

        @pl.when(d == n_dev - 1)
        def _():
            field[:, :, 24:32, :] = jnp.zeros((GX, 2, 8, 128), F32)

    own_coarse(kc, km, 4)

    pl.semaphore_wait(barrier, n_dev - 1 + 6)
    h_conc = halo(0, c0, ysc, yrc, 32, 4, 4)
    h_label = halo(1, lb, ysl, yrl, 32, 3, 3)
    all_send(lists, lrecv, ls_sem, lr_sem)

    def conc_at(src, dst, x, r0, r1):
        _, s = stencil(src, x, r0, r1, 1.0)
        for h in range(2):
            v = cc[x, h, r0:r1, :] + dd[x, h, r0:r1, :] * s[h]
            if dst is None:
                conc_out[x - 4, r0 - 8 : r1 - 8, 128 * h : 128 * h + 128] = v
            else:
                dst[x, h, r0:r1, :] = v

    steps = ((c0, ca), (ca, cb), (cb, cd), (cd, None))
    for k, (src, dst) in enumerate(steps):
        each(5 + k, 35 - k, 15 - k, lambda x, src=src, dst=dst: conc_at(src, dst, x, 8, 40))
    for k in (6, 7):
        loads[k].wait()
    all_wait(lists, lrecv, ls_sem, lr_sem)

    def count(s, carry):
        total = carry
        for r in range(2):
            owner, block = lrecv[s, 0, r], lrecv[s, 1, r]
            place = jnp.where(owner == d, (block & 1) * 32 + ((block >> 1) & 31), -1)
            column = block >> 6
            rows = (lax.broadcasted_iota(jnp.int32, (64, 128), 0) == place).astype(jnp.bfloat16)
            cols = (lax.broadcasted_iota(jnp.int32, (32, 128), 0) == column).astype(jnp.bfloat16)
            total = total + lax.dot_general(
                rows, cols, (((1,), (1,)), ((), ())), preferred_element_type=F32
            )
        return total

    counts = lax.fori_loop(0, n_dev, count, jnp.zeros((64, 32), F32), unroll=8)
    named = jnp.where(counts > 0.0, 1.0, 0.0).astype(jnp.bfloat16)
    spread = (
        lax.broadcasted_iota(jnp.int32, (32, 4096), 1) // 128 == lax.broadcasted_iota(jnp.int32, (32, 4096), 0)
    ).astype(jnp.bfloat16)
    msk[...] = jnp.dot(named, spread, preferred_element_type=F32)
    arrive(h_conc)
    unpack(c0, yrc, 32, 4, 4, True)
    arrive(h_label)
    unpack(lb, yrl, 32, 3, 3, False)
    h_phi = halo(2, ph, ysp, yrp, 32, 3, 3)
    x_kc = coarse_exchange(kc, 0)
    each(1, 4, 3, lambda x: conc_coeffs(x, 0, 48), lambda x: conc_coeffs(x + 35, 0, 48))
    each(4, 36, 8, lambda x: conc_coeffs(x, 0, 8), lambda x: conc_coeffs(x, 40, 48))
    for k, (src, dst) in enumerate(steps):
        r0, r1, low, high = (4, 44, (4, 12), (36, 44)) if k < 3 else (8, 40, (8, 16), (32, 40))
        each(
            1 + k, 5 + k, 4,
            lambda x, src=src, dst=dst, r0=r0, r1=r1: conc_at(src, dst, x, r0, r1),
            lambda x, src=src, dst=dst, r0=r0, r1=r1, k=k: conc_at(src, dst, x + 34 - 2 * k, r0, r1),
        )
        each(
            5 + k, 35 - k, 15 - k,
            lambda x, src=src, dst=dst, low=low: conc_at(src, dst, x, *low),
            lambda x, src=src, dst=dst, high=high: conc_at(src, dst, x, *high),
        )

    def flux_at(x, r0, r1):
        for h in range(2):
            con = conc_out[x, r0:r1, 128 * h : 128 * h + 128]
            u = 0.5 * (sp[x, h, r0:r1, :] - ph[4 + x, h, 8 + r0 : 8 + r1, :]) - 0.1 * jnp.log(con)
            kin = lookup(lb[4 + x, h, 8 + r0 : 8 + r1, :], (0.2, 1.0, 0.5)) * jnp.sqrt(con)
            val = kin * (jnp.exp(u) - jnp.exp(-u))
            val = msk[32 * h + r0 : 32 * h + r1, 128 * x : 128 * x + 128] * val
            fx[4 + x, h, 8 + r0 : 8 + r1, :] = val
            flux_out[x, r0:r1, 128 * h : 128 * h + 128] = val

    for x in range(32):
        if x in (0, 1, 30, 31):
            flux_at(x, 0, 32)
        else:
            flux_at(x, 0, 8)
            flux_at(x, 24, 32)
    pack(fx, ysf, 32, 2)
    h_flux = halo(4, fx, ysf, yrf, 32, 2, 2)
    for x in range(2, 30):
        flux_at(x, 8, 24)

    each(2, 4, 2, lambda x: pot_coeffs(x, 0, 48), lambda x: pot_coeffs(x + 34, 0, 48))
    each(4, 36, 8, lambda x: pot_coeffs(x, 0, 8), lambda x: pot_coeffs(x, 40, 48))
    arrive(h_phi)
    unpack(ph, yrp, 32, 3, 3, True)

    def first(x, carry):
        v, s = stencil(ph, x, 4, 44, 1.0)
        for h in range(2):
            rd = bb[x, h, 4:44, :]
            qq[x, h, 4:44, :] = (0.2 + 0.05 * rd) * v[h] + gg[x, h, 4:44, :] * s[h]
        return carry

    lax.fori_loop(2, 38, first, 0, unroll=12)

    def second(x, r0, r1):
        for h in range(2):
            rd = bb[x, h, r0:r1, :]
            fl = fx[x, h, r0:r1, :]
            ca[x, h, r0:r1, :] = qq[x, h, r0:r1, :] + rd * fl
            src = 0.05 * ph[x, h, r0:r1, :] + fl
            qq[x, h, r0:r1, :] = src
            bb[x, h, r0:r1, :] = rd * src

    def smooth(x, r0, r1):
        v, s = stencil(ca, x, r0, r1, 1.0)
        for h in range(2):
            p2[x, h, r0:r1, :] = 0.2 * v[h] + bb[x, h, r0:r1, :] + gg[x, h, r0:r1, :] * s[h]

    def resid(x, r0, r1):
        v, s = stencil(p2, x, r0, r1, 1.0)
        for h in range(2):
            rs[x - 4, h, r0 - 8 : r1 - 8, :] = (
                qq[x, h, r0:r1, :] - 0.05 * v[h] - kk[x, h, r0:r1, :] * (6.0 * v[h] - s[h])
            )

    each(4, 36, 8, lambda x: second(x, 8, 40))
    each(5, 35, 15, lambda x: smooth(x, 8, 40))
    each(6, 34, 14, lambda x: resid(x, 8, 40))
    arrive(x_kc)
    coarse_edges(kc)

    def coarse_coeffs(x, carry):
        for h in range(2):
            con = kc[x, h, 8:32, :]
            rd = 0.8 / (0.05 + 2.25 * con)
            rc[x, h, 8:32, :] = rd
            gc[x, h, 8:32, :] = rd * con
            wa[x, h, 8:32, :] = jnp.ones((24, 128), F32)
            ka[x, h, 8:32, :] = con
        return carry

    lax.fori_loop(1, 9, coarse_coeffs, 0, unroll=4)

    def dual(w_in, k_in, w_out, k_out):
        def one(x, carry):
            v, s = stencil(k_in, x, 8, 32, 0.0625)
            for h in range(2):
                w = w_in[x, h, 8:32, :]
                w = w - rc[x, h, 8:32, :] * (0.05 * w + 2.25 * v[h] - s[h])
                w_out[x, h, 8:32, :] = w
                k_out[x, h, 8:32, :] = kc[x, h, 8:32, :] * w
            return carry

        lax.fori_loop(1, 9, one, 0, unroll=8)

    for k in range(4):
        dual(wa, ka, wb, kb)
        dual(wb, kb, wa, ka)

    load = jnp.zeros((8, 128), F32)
    row = lax.broadcasted_iota(jnp.int32, (8, 128), 0)
    lane8 = lax.broadcasted_iota(jnp.int32, (8, 128), 1)
    edge_y = jnp.where(((row == 0) & (d == 0)) | ((row == 7) & (d == n_dev - 1)), 1.0, 0.0)
    for x in range(8):
        for h in range(2):
            edge_z = jnp.where(lane8 == 127 * h, 1.0, 0.0)
            edge_xy = edge_y + (1.0 if x in (0, 7) else 0.0)
            load = load + (0.05 + kc[1 + x, h, 16:24, :] * (0.0625 * edge_xy + edge_z))
    load = jnp.sum(load, axis=0, keepdims=True)
    row2 = lax.broadcasted_iota(jnp.int32, (2, 128), 0)

    arrive(h_flux)
    unpack(fx, yrf, 32, 2, 2, True)
    h_km = halo(3, km, ysk, yrk, 16, 2, 2)
    each(2, 4, 2, lambda x: second(x, 4, 44), lambda x: second(x + 34, 4, 44))
    each(4, 36, 8, lambda x: second(x, 0, 8), lambda x: second(x, 40, 48))
    each(3, 5, 2, lambda x: smooth(x, 4, 44), lambda x: smooth(x + 32, 4, 44))
    each(5, 35, 15, lambda x: smooth(x, 4, 12), lambda x: smooth(x, 36, 44))
    each(4, 6, 2, lambda x: resid(x, 8, 40), lambda x: resid(x + 30, 8, 40))
    each(6, 34, 14, lambda x: resid(x, 8, 16), lambda x: resid(x, 32, 40))

    def down(i, carry):
        for h in range(2):
            total = jnp.zeros((16, 128), F32)
            for x in (0, 1):
                for r in (0, 1):
                    total = total + rs[2 * i + x, h, pl.ds(r, 16, stride=2), :]
            sm[4 + i, h, 8:24, :] = 0.25 * total
        return carry

    lax.fori_loop(0, 16, down, 0, unroll=8)
    pack(sm, yss, 16, 2)
    h_sm = halo(5, sm, yss, yrs, 16, 2, 2)
    pack(p2, ysu, 32, 1, 1)
    arrive(h_km)
    unpack(km, yrk, 16, 2, 2, True)

    def mid_coeffs(x, carry):
        for h in range(2):
            con = km[x, h, 4:28, :]
            rd = 0.8 / (0.05 + 3.0 * con)
            bm[x, h, 4:28, :] = rd
            gm[x, h, 4:28, :] = rd * con
        return carry

    lax.fori_loop(2, 22, mid_coeffs, 0, unroll=5)
    h_p2 = halo(7, p2, ysu, yru, 32, 1, 1, 1, False)
    arrive(h_sm)
    unpack(sm, yrs, 16, 2, 2, True)

    def mid_first(x, carry):
        for h in range(2):
            v = bm[x, h, 4:28, :] * sm[x, h, 4:28, :]
            bm[x, h, 4:28, :] = v
            m1[x, h, 4:28, :] = v
        return carry

    lax.fori_loop(2, 22, mid_first, 0, unroll=10)
    sweep(m1, m2, gm, bm, 3, 21, 4, 28, 0.25, 18)

    def mid_resid(x, carry):
        v, s = stencil(m2, x, 8, 24, 0.25)
        for h in range(2):
            m1[x, h, 8:24, :] = sm[x, h, 8:24, :] - 0.05 * v[h] - km[x, h, 8:24, :] * (3.0 * v[h] - s[h])
            mu[x, h, 8:24, :] = v[h]
        return carry

    lax.fori_loop(4, 20, mid_resid, 0, unroll=16)

    own_coarse(sc, m1, 4)
    x_sc = coarse_exchange(sc, 1)
    part = jnp.zeros((8, 128), F32)
    for x in range(8):
        for h in range(2):
            part = part + wa[1 + x, h, 16:24, :] * sc[1 + x, h, 16:24, :]
    part = jnp.sum(part, axis=0, keepdims=True)
    message = jnp.where(row2 == 0, jnp.broadcast_to(part, (2, 128)), jnp.broadcast_to(load, (2, 128)))
    psend[...] = message
    precv[d] = message
    all_send(psend, precv, ps_sem, pr_sem)
    pack(mu, ysm, 16, 3)
    arrive(x_sc)
    coarse_edges(sc)
    h_mu = halo(8, mu, ysm, yrm, 16, 3, 3)

    def coarse_first(x, carry):
        for h in range(2):
            v = rc[x, h, 8:32, :] * sc[x, h, 8:32, :]
            rc[x, h, 8:32, :] = v
            ea[x, h, 8:32, :] = v
        return carry

    lax.fori_loop(1, 9, coarse_first, 0, unroll=8)
    for k in range(3):
        sweep(ea, eb, gc, rc, 1, 9, 8, 32, 0.0625, 8)
        sweep(eb, ea, gc, rc, 1, 9, 8, 32, 0.0625, 8)
    sweep(ea, eb, gc, rc, 1, 9, 8, 32, 0.0625, 8)
    for x in range(8):
        for h in range(2):
            ec[4 + x, h, 8:16, :] = eb[1 + x, h, 16:24, :]
    pack(ec, yse, 8, 2)
    h_ec = halo(6, ec, yse, yre, 8, 2, 2)
    all_wait(psend, precv, ps_sem, pr_sem)

    def gather(s, carry):
        return carry + precv[s]

    sums = lax.fori_loop(0, n_dev, gather, jnp.zeros((2, 128), F32), unroll=8)
    sums = jnp.sum(sums, axis=1, keepdims=True)
    shifts[1] = jnp.broadcast_to(sums[0:1] / sums[1:2], (8, 128))
    x_shift = []
    for k, (t, i) in enumerate((((gd, d), 2), ((gu, d), 0))):
        x_shift.append(
            pltpu.make_async_remote_copy(
                src_ref=shifts.at[1], dst_ref=shifts.at[i], send_sem=ss_sem.at[k], recv_sem=sr_sem.at[k],
                device_id=t, device_id_type=MESH,
            )
        )
    for c in x_shift:
        c.start()
    arrive(h_mu)
    sent(h_mu)
    unpack(mu, yrm, 16, 3, 3, True)
    arrive(h_p2)
    sent(h_p2)
    unpack(p2, yru, 32, 1, 1, True, 1, False)
    arrive(h_ec)
    unpack(ec, yre, 8, 2, 2, True)
    arrive(x_shift)

    row12 = lax.broadcasted_iota(jnp.int32, (12, 128), 0)
    inside = jnp.where(((row12 < 2) & (d == 0)) | ((row12 >= 10) & (d == n_dev - 1)), 0.0, 1.0)
    own_shift = inside * shifts[1, 0:1, :]
    low_shift = jnp.where(g == 0, jnp.zeros((12, 128), F32), inside * shifts[0, 0:1, :])
    high_shift = jnp.where(g == n_grp - 1, jnp.zeros((12, 128), F32), inside * shifts[2, 0:1, :])
    for i in range(2, 14):
        for h in range(2):
            v = ec[i, h, 6:18, :] + (low_shift if i < 4 else own_shift if i < 12 else high_shift)
            for x in (0, 1):
                if not 1 <= 2 * i - 4 + x < 23:
                    continue
                for r in (0, 1):
                    rows = pl.ds(4 + r, 12, stride=2)
                    mu[2 * i - 4 + x, h, rows, :] = mu[2 * i - 4 + x, h, rows, :] + v
    sweep(mu, m1, gm, bm, 2, 22, 4, 28, 0.25, 10)
    sweep(m1, m2, gm, bm, 3, 21, 4, 28, 0.25, 18)

    def fine_up(i, carry):
        for h in range(2):
            v = m2[i, h, 6:26, :]
            for x in (0, 1):
                for r in (0, 1):
                    rows = pl.ds(4 + r, 20, stride=2)
                    p2[2 * i - 4 + x, h, rows, :] = p2[2 * i - 4 + x, h, rows, :] + v
        return carry

    lax.fori_loop(3, 21, fine_up, 0, unroll=6)
    sweep(p2, ca, gg, bb, 3, 37, 4, 44, 1.0, 17)

    for copies in (h_conc, h_label, h_phi, h_km, h_flux, h_sm, h_ec, x_kc, x_sc, x_shift):
        sent(copies)


def finish(conc, flux, last, gain, rhs, conc_out, flux_out, pot_out, pot, sem):
    copies = [pltpu.make_async_copy(conc, conc_out, sem.at[4]), pltpu.make_async_copy(flux, flux_out, sem.at[5])]
    for c in copies:
        c.start()

    def one(x, carry):
        v, s = stencil(last, x, 8, 40, 1.0)
        for h in range(2):
            new = 0.2 * v[h] + rhs[x, h, 8:40, :] + gain[x, h, 8:40, :] * s[h]
            pot[x - 4, :, 128 * h : 128 * h + 128] = new
        return carry

    for k in range(4):
        lax.fori_loop(4 + 8 * k, 12 + 8 * k, one, 0, unroll=8)
        part = pl.ds(8 * k, 8)
        copies.append(pltpu.make_async_copy(pot.at[part], pot_out.at[part], sem.at[k]))
        copies[-1].start()
    for c in copies:
        c.wait()


def body(conc_old, phi_old, solid_pot, phase_label, iface_block, iface_owner):
    n_grp, n_dev = lax.axis_size("grp"), lax.axis_size("dev")
    fine = pltpu.VMEM((FX, 2, FY, 128), F32)
    mid = pltpu.VMEM((MX, 2, MY, 128), F32)
    coarse = pltpu.VMEM((GX, 2, GY, 128), F32)
    dma = pltpu.SemaphoreType.DMA
    out = jax.ShapeDtypeStruct(conc_old.shape, F32)
    kept = pltpu.VMEM(conc_old.shape, F32)
    hbm = pl.BlockSpec(memory_space=pltpu.HBM)
    vmem = pl.BlockSpec(memory_space=pltpu.VMEM)

    def faces(n, deep, dtype=F32):
        c = 8 * ((4 * deep + 7) // 8)
        return [pltpu.VMEM((2, 2, n * deep, 128), dtype), pltpu.VMEM((2, 2, n * deep + 2 * c, 128), dtype)]

    arguments = (conc_old, phi_old, solid_pot, phase_label, iface_owner.reshape(1, 256), iface_block)
    fields = pl.pallas_call(
        functools.partial(kernel, n_grp, n_dev),
        out_shape=(kept, kept, fine, fine, fine),
        in_specs=[hbm] * 6,
        out_specs=(vmem,) * 5,
        scratch_shapes=[
            fine, pltpu.VMEM((FX, 2, FY, 128), jnp.int32), fine, pltpu.VMEM((32, 2, 32, 128), F32),
            fine, fine, pltpu.VMEM((32, 2, 32, 128), F32), fine, fine, fine, fine, fine, fine,
            mid, mid, mid, mid, mid, mid, mid,
            coarse, coarse, coarse, coarse, coarse, coarse, coarse, coarse, coarse, coarse,
            pltpu.VMEM((EX, 2, EY, 128), F32),
            *faces(32, 4), *faces(32, 3, jnp.int32), *faces(32, 3), *faces(32, 2), *faces(32, 1),
            *faces(16, 2), *faces(16, 2), *faces(16, 3), *faces(8, 2),
            pltpu.VMEM((2, 2, 1, 128), jnp.int32), pltpu.VMEM((n_dev, 2, 2, 1, 128), jnp.int32), pltpu.VMEM((64, 4096), F32),
            pltpu.VMEM((2, 128), F32), pltpu.VMEM((n_dev, 2, 128), F32), pltpu.VMEM((3, 8, 128), F32),
            dma((12,)), dma((9, 8)), dma((9, 8)), dma((2, 2)), dma((2, 2)),
            dma((n_dev,)), dma((n_dev,)), dma((n_dev,)), dma((n_dev,)), dma((2,)), dma((2,)),
        ],
        compiler_params=pltpu.CompilerParams(
            collective_id=0, has_side_effects=True, vmem_limit_bytes=43 * 1024 * 1024
        ),
    )(*[pltpu.with_memory_space_constraint(argument, pltpu.HBM) for argument in arguments])
    return pl.pallas_call(
        finish,
        out_shape=(out, out, out),
        in_specs=[vmem] * 5,
        out_specs=(hbm, hbm, hbm),
        scratch_shapes=[pltpu.VMEM(conc_old.shape, F32), dma((6,))],
        compiler_params=pltpu.CompilerParams(vmem_limit_bytes=8 * 1024 * 1024),
    )(*[pltpu.with_memory_space_constraint(field, pltpu.VMEM) for field in fields])


def solution(mesh):
    split = P("grp", "dev", None)
    return jax.shard_map(
        body,
        mesh=mesh,
        in_specs=(split, split, split, split, P("grp", "dev"), split),
        out_specs=(split, split, split),
        check_vma=False,
    )
```

```python
import functools

import jax
import jax.numpy as jnp
from jax import lax
from jax.experimental import pallas as pl
from jax.experimental.pallas import tpu as pltpu
from jax.sharding import PartitionSpec as P

MESH = pl.DeviceIdType.MESH
F32 = jnp.float32

FX, FY = 40, 48
MX, MY = 24, 32
EX, EY = 16, 24
GX, GY = 10, 40


def lookup(label, table):
    return jnp.where(label == 0, table[0], jnp.where(label == 1, table[1], table[2])).astype(F32)


def z_sum(a, b):
    lane = lax.broadcasted_iota(jnp.int32, (1, 128), 1)
    l0, l1 = lane == 0, lane == 127
    ra, rb = pltpu.roll(a, 1, 1), pltpu.roll(b, 1, 1)
    sa, sb = pltpu.roll(a, 127, 1), pltpu.roll(b, 127, 1)
    zero = jnp.zeros_like(a)
    za = jnp.where(l0, zero, ra) + jnp.where(l1, sb, sa)
    zb = jnp.where(l0, ra, rb) + jnp.where(l1, zero, sb)
    return za, zb


def plane(field, x, h, r0, r1):
    return (field[x - 1, h, r0:r1, :] + field[x + 1, h, r0:r1, :]) + (
        field[x, h, r0 - 1 : r1 - 1, :] + field[x, h, r0 + 1 : r1 + 1, :]
    )


def stencil(field, x, r0, r1, weight):
    a, b = field[x, 0, r0:r1, :], field[x, 1, r0:r1, :]
    za, zb = z_sum(a, b)
    pa, pb = plane(field, x, 0, r0, r1), plane(field, x, 1, r0, r1)
    if weight != 1.0:
        pa, pb = weight * pa, weight * pb
    return (a, b), (pa + za, pb + zb)


def kernel(
    n_grp,
    n_dev,
    conc_hbm,
    phi_hbm,
    solid_hbm,
    label_hbm,
    owner_hbm,
    block_hbm,
    conc_out,
    flux_out,
    ca,
    gg,
    bb,
    c0, lb, ph, sp, cb, cd, rs, dd, cc, kk, qq, fx, p2,
    sm, km, gm, bm, m1, m2, mu,
    kc, rc, gc, wa, wb, ka, kb, sc, ea, eb,
    ec,
    ysc, yrc, ysl, yrl, ysp, yrp, ysf, yrf, ysu, yru, ysk, yrk, yss, yrs, ysm, yrm, yse, yre,
    lists, lsend, lrecv, msk, psend, precv, shifts,
    in_sem, hs_sem, hr_sem, cs_sem, cr_sem, ls_sem, lr_sem, ps_sem, pr_sem, ss_sem, sr_sem,
):
    g = lax.axis_index("grp")
    d = lax.axis_index("dev")
    gu, gd = lax.rem(g + 1, n_grp), lax.rem(g + n_grp - 1, n_grp)
    du, dl = lax.rem(d + 1, n_dev), lax.rem(d + n_dev - 1, n_dev)
    eight = [(gd, dl), (gd, d), (gd, du), (g, dl), (g, du), (gu, dl), (gu, d), (gu, du)]

    loads = []
    for k, (src, dst) in enumerate(((conc_hbm, c0), (label_hbm, lb), (phi_hbm, ph))):
        for h in range(2):
            loads.append(
                pltpu.make_async_copy(
                    src.at[:, :, pl.ds(128 * h, 128)], dst.at[pl.ds(4, 32), h, pl.ds(8, 32), :], in_sem.at[2 * k + h]
                )
            )
    for h in range(2):
        loads.append(
            pltpu.make_async_copy(solid_hbm.at[:, :, pl.ds(128 * h, 128)], sp.at[:, h], in_sem.at[6 + h])
        )
    for k, src in enumerate((owner_hbm, block_hbm)):
        for r in range(2):
            loads.append(
                pltpu.make_async_copy(src.at[:, pl.ds(128 * r, 128)], lists.at[k, r], in_sem.at[8 + 2 * k + r])
            )
    for load in loads:
        load.start()

    barrier = pltpu.get_barrier_semaphore()
    for t in (eight[0], eight[1], eight[2], eight[5], eight[6], eight[7]):
        pl.semaphore_signal(barrier, inc=1, device_id=t, device_id_type=MESH)

    def greet(j, carry):
        pl.semaphore_signal(barrier, inc=1, device_id=(g, lax.rem(d + j, n_dev)), device_id_type=MESH)
        return carry

    lax.fori_loop(1, n_dev, greet, 0)

    for ref, rows in ((kc, (0, 8, 32, 40)), (sc, (0, 8, 32, 40)), (ka, (0, 8, 32, 40)), (kb, (0, 8, 32, 40)), (ea, (0, 8, 32, 40)), (eb, (0, 8, 32, 40))):
        ref[:, :, 0:8, :] = jnp.zeros((GX, 2, 8, 128), F32)
        ref[:, :, 32:40, :] = jnp.zeros((GX, 2, 8, 128), F32)
        ref[0] = jnp.zeros((2, GY, 128), F32)
        ref[GX - 1] = jnp.zeros((2, GY, 128), F32)

    def pack(field, ys, n, deep, off=0):
        def one(x, carry):
            for s, r in ((0, 8 + off), (1, 8 + n - deep - off)):
                for h in range(2):
                    ys[s, h, pl.ds(deep * x, deep), :] = field[4 + x, h, r : r + deep, :]
            return carry

        lax.fori_loop(0, n, one, 0, unroll=8)

    def unpack(field, yr, n, deep, wide, zero, off=0, corners=True):
        edge_rows = 8 * ((4 * deep + 7) // 8)

        def one(x, carry):
            for s, r, edge in ((0, 8 - deep - off, d == 0), (1, 8 + n + off, d == n_dev - 1)):
                for h in range(2):
                    v = yr[s, h, pl.ds(edge_rows + deep * (x - 4), deep), :]
                    field[x, h, r : r + deep, :] = jnp.where(edge, jnp.zeros_like(v), v)
            return carry

        reach = wide if corners else 0
        lax.fori_loop(4 - reach, 4 + n + reach, one, 0, unroll=8)
        if zero:
            @pl.when(g == 0)
            def _():
                field[4 - wide - off : 4 - off] = jnp.zeros(field.at[4 - wide : 4].shape, field.dtype)

            @pl.when(g == n_grp - 1)
            def _():
                field[4 + n + off : 4 + n + wide + off] = jnp.zeros(field.at[4 - wide : 4].shape, field.dtype)

    def halo(e, field, ys, yr, n, deep, wide, off=0, corners=True):
        c = 8 * ((4 * deep + 7) // 8)
        m = n * deep
        own = pl.ds(8, n)
        low, high = field.at[pl.ds(4 + off, wide), :, own, :], field.at[pl.ds(4 + n - wide - off, wide), :, own, :]
        to_low, to_high = field.at[pl.ds(4 - wide - off, wide), :, own, :], field.at[pl.ds(4 + n + off, wide), :, own, :]
        first, last, after, before = pl.ds(0, c), pl.ds(m - c, c), pl.ds(c + m, c), pl.ds(0, c)
        pairs = [
            (ys.at[0, :, first], yr.at[1, :, after]),
            (low, to_high),
            (ys.at[1, :, first], yr.at[0, :, after]),
            (ys.at[0], yr.at[1, :, pl.ds(c, m)]),
            (ys.at[1], yr.at[0, :, pl.ds(c, m)]),
            (ys.at[0, :, last], yr.at[1, :, before]),
            (high, to_low),
            (ys.at[1, :, last], yr.at[0, :, before]),
        ]
        copies = []
        for i in (0, 2, 5, 7, 4, 3, 6, 1) if corners else (4, 3, 6, 1):
            src, dst = pairs[i]
            copies.append(
                pltpu.make_async_remote_copy(
                    src_ref=src, dst_ref=dst, send_sem=hs_sem.at[e, i], recv_sem=hr_sem.at[e, i],
                    device_id=eight[i], device_id_type=MESH,
                )
            )
        for c in copies:
            c.start()
        return copies

    def sent(copies):
        for c in copies:
            c.wait_send()

    def arrive(copies):
        for c in copies:
            c.wait_recv()

    def all_send(src, dst, send_sem, recv_sem):
        def one(j, carry):
            pltpu.make_async_remote_copy(
                src_ref=src.at[lax.rem(d + j, n_dev)] if src.shape[0] == n_dev else src, dst_ref=dst.at[d], send_sem=send_sem.at[j], recv_sem=recv_sem.at[d],
                device_id=(g, lax.rem(d + j, n_dev)), device_id_type=MESH,
            ).start()
            return carry

        lax.fori_loop(1, n_dev, one, 0)

    def all_wait(src, dst, send_sem, recv_sem):
        def one(j, carry):
            s = lax.rem(d + n_dev - j, n_dev)
            c = pltpu.make_async_remote_copy(
                src_ref=src.at[lax.rem(d + j, n_dev)] if src.shape[0] == n_dev else src, dst_ref=dst.at[s], send_sem=send_sem.at[j], recv_sem=recv_sem.at[s],
                device_id=(g, lax.rem(d + j, n_dev)), device_id_type=MESH,
            )
            c.wait_recv()
            c.wait_send()
            return carry

        lax.fori_loop(1, n_dev, one, 0)

    def sweep(src, dst, gain, rhs, x0, x1, r0, r1, weight, unroll):
        def one(x, carry):
            v, s = stencil(src, x, r0, r1, weight)
            for h in range(2):
                dst[x, h, r0:r1, :] = 0.2 * v[h] + rhs[x, h, r0:r1, :] + gain[x, h, r0:r1, :] * s[h]
            return carry

        lax.fori_loop(x0, x1, one, 0, unroll=unroll)

    for k in range(4):
        loads[k].wait()
    pack(c0, ysc, 32, 4)
    pack(lb, ysl, 32, 3)

    def conc_coeffs(x, r0, r1):
        for h in range(2):
            old = c0[x, h, r0:r1, :]
            label = lb[x, h, r0:r1, :]
            dd[x, h, r0:r1, :] = jnp.where(old > 0.0, lookup(label, (1.5 / 10.0, 0.1 / 1.6, 0.4 / 3.4)), 0.0)
            cc[x, h, r0:r1, :] = old * lookup(label, (1.0 / 10.0, 1.0 / 1.6, 1.0 / 3.4))

    def pot_coeffs(x, r0, r1):
        for h in range(2):
            con = lookup(lb[x, h, r0:r1, :], (1.0, 0.3, 0.6)) * c0[x, h, r0:r1, :]
            rd = 0.8 / (0.05 + 6.0 * con)
            kk[x, h, r0:r1, :] = con
            bb[x, h, r0:r1, :] = rd
            gg[x, h, r0:r1, :] = rd * con

    def each(lo, hi, unroll, *fns):
        def one(x, carry):
            for fn in fns:
                fn(x)
            return carry

        lax.fori_loop(lo, hi, one, 0, unroll=unroll)

    each(4, 36, 4, lambda x: conc_coeffs(x, 8, 40), lambda x: pot_coeffs(x, 8, 40))
    loads[4].wait()
    loads[5].wait()
    pack(ph, ysp, 32, 3)
    for k in range(8, 12):
        loads[k].wait()
    owners = jnp.concatenate([lists[0, 0], lists[0, 1]], axis=1)
    values = jnp.concatenate([lists[1, 0], lists[1, 1]], axis=1) + 1
    onehot = lax.broadcasted_iota(jnp.int32, (n_dev, 256), 0) == owners
    ones = jnp.where(onehot, 1.0, 0.0)
    earlier = lax.broadcasted_iota(jnp.int32, (256, 256), 0) < lax.broadcasted_iota(jnp.int32, (256, 256), 1)
    before = jnp.dot(
        ones.astype(jnp.bfloat16), jnp.where(earlier, 1.0, 0.0).astype(jnp.bfloat16), preferred_element_type=F32
    )
    rank = jnp.sum(ones * before, axis=0, keepdims=True) + (16 * lax.rem(d, 8)).astype(F32)
    slots = lax.broadcasted_iota(jnp.int32, (128, 256), 0).astype(F32) == rank
    slots = jnp.where(slots, 1.0, 0.0).astype(jnp.bfloat16)
    by_owner = jnp.zeros((n_dev, 128), F32)
    for part, scale in ((values >> 6, 64.0), (values & 63, 1.0)):
        terms = jnp.where(onehot, part.astype(F32), 0.0).astype(jnp.bfloat16)
        by_owner = by_owner + scale * lax.dot_general(
            terms, slots, (((1,), (1,)), ((), ())), preferred_element_type=F32
        )
    by_owner = by_owner.astype(jnp.int32) - 1
    for o in range(n_dev):
        lsend[o] = by_owner[o : o + 1, :]
    lrecv[d] = lsend[d]

    def own_mid(i, carry):
        for h in range(2):
            total = jnp.zeros((16, 128), F32)
            for x in (0, 1):
                for r in (0, 1):
                    rows = pl.ds(8 + r, 16, stride=2)
                    total = total + kk[4 + 2 * i + x, h, rows, :]
            km[4 + i, h, 8:24, :] = 0.25 * total
        return carry

    lax.fori_loop(0, 16, own_mid, 0, unroll=4)
    pack(km, ysk, 16, 2)

    def own_coarse(dst, src, off):
        def one(i, carry):
            for h in range(2):
                total = jnp.zeros((8, 128), F32)
                for x in (0, 1):
                    for r in (0, 1):
                        total = total + src[off + 2 * i + x, h, pl.ds(8 + r, 8, stride=2), :]
                dst[1 + i, h, 16:24, :] = 0.25 * total
            return carry

        lax.fori_loop(0, 8, one, 0, unroll=8)

    def coarse_exchange(field, k):
        copies = []
        for i, (t, r) in enumerate((((g, dl), 24), ((g, du), 8))):
            copies.append(
                pltpu.make_async_remote_copy(
                    src_ref=field.at[pl.ds(1, 8), :, pl.ds(16, 8), :], dst_ref=field.at[pl.ds(1, 8), :, pl.ds(r, 8), :],
                    send_sem=cs_sem.at[k, i], recv_sem=cr_sem.at[k, i], device_id=t, device_id_type=MESH,
                )
            )
        for c in copies:
            c.start()
        return copies

    def coarse_edges(field):
        @pl.when(d == 0)
        def _():
            field[:, :, 8:16, :] = jnp.zeros((GX, 2, 8, 128), F32)

        @pl.when(d == n_dev - 1)
        def _():
            field[:, :, 24:32, :] = jnp.zeros((GX, 2, 8, 128), F32)

    own_coarse(kc, km, 4)

    pl.semaphore_wait(barrier, n_dev - 1 + 6)
    all_send(lsend, lrecv, ls_sem, lr_sem)
    h_conc = halo(0, c0, ysc, yrc, 32, 4, 4)
    h_label = halo(1, lb, ysl, yrl, 32, 3, 3)

    def conc_at(src, dst, x, r0, r1):
        _, s = stencil(src, x, r0, r1, 1.0)
        for h in range(2):
            v = cc[x, h, r0:r1, :] + dd[x, h, r0:r1, :] * s[h]
            if dst is None:
                conc_out[x - 4, r0 - 8 : r1 - 8, 128 * h : 128 * h + 128] = v
            else:
                dst[x, h, r0:r1, :] = v

    steps = ((c0, ca), (ca, cb), (cb, cd), (cd, None))
    for k, (src, dst) in enumerate(steps):
        each(5 + k, 35 - k, 15 - k, lambda x, src=src, dst=dst: conc_at(src, dst, x, 8, 40))
    for k in (6, 7):
        loads[k].wait()
    all_wait(lsend, lrecv, ls_sem, lr_sem)

    counts = jnp.zeros((64, 32), F32)
    for q in range(n_dev // 8):
        block = lrecv[8 * q]
        for k in range(1, 8):
            block = jnp.maximum(block, lrecv[8 * q + k])
        place = jnp.where(block >= 0, (block & 1) * 32 + ((block >> 1) & 31), -1)
        rows = jnp.where(lax.broadcasted_iota(jnp.int32, (64, 128), 0) == place, 1.0, 0.0).astype(jnp.bfloat16)
        cols = jnp.where(lax.broadcasted_iota(jnp.int32, (32, 128), 0) == block >> 6, 1.0, 0.0).astype(jnp.bfloat16)
        counts = counts + lax.dot_general(rows, cols, (((1,), (1,)), ((), ())), preferred_element_type=F32)
    named = jnp.where(counts > 0.0, 1.0, 0.0).astype(jnp.bfloat16)
    spread = (
        lax.broadcasted_iota(jnp.int32, (32, 4096), 1) // 128 == lax.broadcasted_iota(jnp.int32, (32, 4096), 0)
    ).astype(jnp.bfloat16)
    msk[...] = jnp.dot(named, spread, preferred_element_type=F32)
    arrive(h_conc)
    unpack(c0, yrc, 32, 4, 4, True)
    arrive(h_label)
    unpack(lb, yrl, 32, 3, 3, False)
    h_phi = halo(2, ph, ysp, yrp, 32, 3, 3)
    each(1, 4, 3, lambda x: conc_coeffs(x, 0, 48), lambda x: conc_coeffs(x + 35, 0, 48))
    each(4, 36, 8, lambda x: conc_coeffs(x, 0, 8), lambda x: conc_coeffs(x, 40, 48))
    for k, (src, dst) in enumerate(steps):
        r0, r1, low, high = (4, 44, (4, 12), (36, 44)) if k < 3 else (8, 40, (8, 16), (32, 40))
        each(
            1 + k, 5 + k, 4,
            lambda x, src=src, dst=dst, r0=r0, r1=r1: conc_at(src, dst, x, r0, r1),
            lambda x, src=src, dst=dst, r0=r0, r1=r1, k=k: conc_at(src, dst, x + 34 - 2 * k, r0, r1),
        )
        each(
            5 + k, 35 - k, 15 - k,
            lambda x, src=src, dst=dst, low=low: conc_at(src, dst, x, *low),
            lambda x, src=src, dst=dst, high=high: conc_at(src, dst, x, *high),
        )

    def flux_at(x, r0, r1):
        for h in range(2):
            con = conc_out[x, r0:r1, 128 * h : 128 * h + 128]
            u = 0.5 * (sp[x, h, r0:r1, :] - ph[4 + x, h, 8 + r0 : 8 + r1, :]) - 0.1 * jnp.log(con)
            kin = lookup(lb[4 + x, h, 8 + r0 : 8 + r1, :], (0.2, 1.0, 0.5)) * jnp.sqrt(con)
            val = kin * (jnp.exp(u) - jnp.exp(-u))
            val = msk[32 * h + r0 : 32 * h + r1, 128 * x : 128 * x + 128] * val
            fx[4 + x, h, 8 + r0 : 8 + r1, :] = val
            flux_out[x, r0:r1, 128 * h : 128 * h + 128] = val

    for x in range(32):
        if x in (0, 1, 30, 31):
            flux_at(x, 0, 32)
        else:
            flux_at(x, 0, 8)
            flux_at(x, 24, 32)
    pack(fx, ysf, 32, 2)
    h_flux = halo(4, fx, ysf, yrf, 32, 2, 2)
    for x in range(2, 30):
        flux_at(x, 8, 24)

    each(2, 4, 2, lambda x: pot_coeffs(x, 0, 48), lambda x: pot_coeffs(x + 34, 0, 48))
    each(4, 36, 8, lambda x: pot_coeffs(x, 0, 8), lambda x: pot_coeffs(x, 40, 48))
    arrive(h_phi)
    unpack(ph, yrp, 32, 3, 3, True)

    def first(x, carry):
        v, s = stencil(ph, x, 4, 44, 1.0)
        for h in range(2):
            rd = bb[x, h, 4:44, :]
            qq[x, h, 4:44, :] = (0.2 + 0.05 * rd) * v[h] + gg[x, h, 4:44, :] * s[h]
        return carry

    lax.fori_loop(2, 38, first, 0, unroll=12)

    def second(x, r0, r1):
        for h in range(2):
            rd = bb[x, h, r0:r1, :]
            fl = fx[x, h, r0:r1, :]
            ca[x, h, r0:r1, :] = qq[x, h, r0:r1, :] + rd * fl
            src = 0.05 * ph[x, h, r0:r1, :] + fl
            qq[x, h, r0:r1, :] = src
            bb[x, h, r0:r1, :] = rd * src

    def smooth(x, r0, r1):
        v, s = stencil(ca, x, r0, r1, 1.0)
        for h in range(2):
            p2[x, h, r0:r1, :] = 0.2 * v[h] + bb[x, h, r0:r1, :] + gg[x, h, r0:r1, :] * s[h]

    def resid(x, r0, r1):
        v, s = stencil(p2, x, r0, r1, 1.0)
        for h in range(2):
            rs[x - 4, h, r0 - 8 : r1 - 8, :] = (
                qq[x, h, r0:r1, :] - 0.05 * v[h] - kk[x, h, r0:r1, :] * (6.0 * v[h] - s[h])
            )

    each(4, 36, 8, lambda x: second(x, 8, 40))
    each(5, 35, 15, lambda x: smooth(x, 8, 40))
    each(6, 34, 14, lambda x: resid(x, 8, 40))
    arrive(h_flux)
    unpack(fx, yrf, 32, 2, 2, True)
    h_km = halo(3, km, ysk, yrk, 16, 2, 2)
    x_kc = coarse_exchange(kc, 0)
    each(2, 4, 2, lambda x: second(x, 4, 44), lambda x: second(x + 34, 4, 44))
    each(4, 36, 8, lambda x: second(x, 0, 8), lambda x: second(x, 40, 48))
    each(3, 5, 2, lambda x: smooth(x, 4, 44), lambda x: smooth(x + 32, 4, 44))
    each(5, 35, 15, lambda x: smooth(x, 4, 12), lambda x: smooth(x, 36, 44))
    each(4, 6, 2, lambda x: resid(x, 8, 40), lambda x: resid(x + 30, 8, 40))
    each(6, 34, 14, lambda x: resid(x, 8, 16), lambda x: resid(x, 32, 40))

    def down(i, carry):
        for h in range(2):
            total = jnp.zeros((16, 128), F32)
            for x in (0, 1):
                for r in (0, 1):
                    total = total + rs[2 * i + x, h, pl.ds(r, 16, stride=2), :]
            sm[4 + i, h, 8:24, :] = 0.25 * total
        return carry

    lax.fori_loop(0, 16, down, 0, unroll=8)
    pack(sm, yss, 16, 2)
    h_sm = halo(5, sm, yss, yrs, 16, 2, 2)
    pack(p2, ysu, 32, 1, 1)
    arrive(h_km)
    unpack(km, yrk, 16, 2, 2, True)

    def mid_coeffs(x, carry):
        for h in range(2):
            con = km[x, h, 4:28, :]
            rd = 0.8 / (0.05 + 3.0 * con)
            bm[x, h, 4:28, :] = rd
            gm[x, h, 4:28, :] = rd * con
        return carry

    lax.fori_loop(2, 22, mid_coeffs, 0, unroll=5)
    h_p2 = halo(7, p2, ysu, yru, 32, 1, 1, 1, False)
    arrive(x_kc)
    coarse_edges(kc)

    def coarse_coeffs(x, carry):
        for h in range(2):
            con = kc[x, h, 8:32, :]
            rd = 0.8 / (0.05 + 2.25 * con)
            rc[x, h, 8:32, :] = rd
            gc[x, h, 8:32, :] = rd * con
            wa[x, h, 8:32, :] = jnp.ones((24, 128), F32)
            ka[x, h, 8:32, :] = con
        return carry

    lax.fori_loop(1, 9, coarse_coeffs, 0, unroll=4)

    def dual(w_in, k_in, w_out, k_out):
        def one(x, carry):
            v, s = stencil(k_in, x, 8, 32, 0.0625)
            for h in range(2):
                w = w_in[x, h, 8:32, :]
                w = w - rc[x, h, 8:32, :] * (0.05 * w + 2.25 * v[h] - s[h])
                w_out[x, h, 8:32, :] = w
                k_out[x, h, 8:32, :] = kc[x, h, 8:32, :] * w
            return carry

        lax.fori_loop(1, 9, one, 0, unroll=8)

    for k in range(4):
        dual(wa, ka, wb, kb)
        dual(wb, kb, wa, ka)

    load = jnp.zeros((8, 128), F32)
    row = lax.broadcasted_iota(jnp.int32, (8, 128), 0)
    lane8 = lax.broadcasted_iota(jnp.int32, (8, 128), 1)
    edge_y = jnp.where(((row == 0) & (d == 0)) | ((row == 7) & (d == n_dev - 1)), 1.0, 0.0)
    for x in range(8):
        for h in range(2):
            edge_z = jnp.where(lane8 == 127 * h, 1.0, 0.0)
            edge_xy = edge_y + (1.0 if x in (0, 7) else 0.0)
            load = load + (0.05 + kc[1 + x, h, 16:24, :] * (0.0625 * edge_xy + edge_z))
    load = jnp.sum(load, axis=0, keepdims=True)
    row2 = lax.broadcasted_iota(jnp.int32, (2, 128), 0)

    arrive(h_sm)
    unpack(sm, yrs, 16, 2, 2, True)

    def mid_first(x, carry):
        for h in range(2):
            v = bm[x, h, 4:28, :] * sm[x, h, 4:28, :]
            bm[x, h, 4:28, :] = v
            m1[x, h, 4:28, :] = v
        return carry

    lax.fori_loop(2, 22, mid_first, 0, unroll=10)
    sweep(m1, m2, gm, bm, 3, 21, 4, 28, 0.25, 18)

    def mid_resid(x, carry):
        v, s = stencil(m2, x, 8, 24, 0.25)
        for h in range(2):
            m1[x, h, 8:24, :] = sm[x, h, 8:24, :] - 0.05 * v[h] - km[x, h, 8:24, :] * (3.0 * v[h] - s[h])
            mu[x, h, 8:24, :] = v[h]
        return carry

    lax.fori_loop(4, 20, mid_resid, 0, unroll=16)

    own_coarse(sc, m1, 4)
    x_sc = coarse_exchange(sc, 1)
    part = jnp.zeros((8, 128), F32)
    for x in range(8):
        for h in range(2):
            part = part + wa[1 + x, h, 16:24, :] * sc[1 + x, h, 16:24, :]
    part = jnp.sum(part, axis=0, keepdims=True)
    message = jnp.where(row2 == 0, jnp.broadcast_to(part, (2, 128)), jnp.broadcast_to(load, (2, 128)))
    psend[...] = message
    precv[d] = message
    all_send(psend, precv, ps_sem, pr_sem)
    pack(mu, ysm, 16, 3)
    arrive(x_sc)
    coarse_edges(sc)
    h_mu = halo(8, mu, ysm, yrm, 16, 3, 3)

    def coarse_first(x, carry):
        for h in range(2):
            v = rc[x, h, 8:32, :] * sc[x, h, 8:32, :]
            rc[x, h, 8:32, :] = v
            ea[x, h, 8:32, :] = v
        return carry

    lax.fori_loop(1, 9, coarse_first, 0, unroll=8)
    for k in range(3):
        sweep(ea, eb, gc, rc, 1, 9, 8, 32, 0.0625, 8)
        sweep(eb, ea, gc, rc, 1, 9, 8, 32, 0.0625, 8)
    sweep(ea, eb, gc, rc, 1, 9, 8, 32, 0.0625, 8)
    for x in range(8):
        for h in range(2):
            ec[4 + x, h, 8:16, :] = eb[1 + x, h, 16:24, :]
    pack(ec, yse, 8, 2)
    h_ec = halo(6, ec, yse, yre, 8, 2, 2)
    all_wait(psend, precv, ps_sem, pr_sem)

    def gather(s, carry):
        return carry + precv[s]

    sums = lax.fori_loop(0, n_dev, gather, jnp.zeros((2, 128), F32), unroll=8)
    sums = jnp.sum(sums, axis=1, keepdims=True)
    shifts[1] = jnp.broadcast_to(sums[0:1] / sums[1:2], (8, 128))
    x_shift = []
    for k, (t, i) in enumerate((((gd, d), 2), ((gu, d), 0))):
        x_shift.append(
            pltpu.make_async_remote_copy(
                src_ref=shifts.at[1], dst_ref=shifts.at[i], send_sem=ss_sem.at[k], recv_sem=sr_sem.at[k],
                device_id=t, device_id_type=MESH,
            )
        )
    for c in x_shift:
        c.start()
    arrive(h_mu)
    sent(h_mu)
    unpack(mu, yrm, 16, 3, 3, True)
    arrive(h_p2)
    sent(h_p2)
    unpack(p2, yru, 32, 1, 1, True, 1, False)
    arrive(h_ec)
    unpack(ec, yre, 8, 2, 2, True)
    arrive(x_shift)

    row12 = lax.broadcasted_iota(jnp.int32, (12, 128), 0)
    inside = jnp.where(((row12 < 2) & (d == 0)) | ((row12 >= 10) & (d == n_dev - 1)), 0.0, 1.0)
    own_shift = inside * shifts[1, 0:1, :]
    low_shift = jnp.where(g == 0, jnp.zeros((12, 128), F32), inside * shifts[0, 0:1, :])
    high_shift = jnp.where(g == n_grp - 1, jnp.zeros((12, 128), F32), inside * shifts[2, 0:1, :])
    for i in range(2, 14):
        for h in range(2):
            v = ec[i, h, 6:18, :] + (low_shift if i < 4 else own_shift if i < 12 else high_shift)
            for x in (0, 1):
                if not 1 <= 2 * i - 4 + x < 23:
                    continue
                for r in (0, 1):
                    rows = pl.ds(4 + r, 12, stride=2)
                    mu[2 * i - 4 + x, h, rows, :] = mu[2 * i - 4 + x, h, rows, :] + v
    sweep(mu, m1, gm, bm, 2, 22, 4, 28, 0.25, 10)
    sweep(m1, m2, gm, bm, 3, 21, 4, 28, 0.25, 18)

    def fine_up(i, carry):
        for h in range(2):
            v = m2[i, h, 6:26, :]
            for x in (0, 1):
                for r in (0, 1):
                    rows = pl.ds(4 + r, 20, stride=2)
                    p2[2 * i - 4 + x, h, rows, :] = p2[2 * i - 4 + x, h, rows, :] + v
        return carry

    lax.fori_loop(3, 21, fine_up, 0, unroll=6)
    sweep(p2, ca, gg, bb, 3, 37, 4, 44, 1.0, 17)

    for copies in (h_conc, h_label, h_phi, h_km, h_flux, h_sm, h_ec, x_kc, x_sc, x_shift):
        sent(copies)


def finish(conc, flux, last, gain, rhs, conc_out, flux_out, pot_out, pot, sem):
    copies = [pltpu.make_async_copy(conc, conc_out, sem.at[4]), pltpu.make_async_copy(flux, flux_out, sem.at[5])]
    for c in copies:
        c.start()

    def one(x, carry):
        v, s = stencil(last, x, 8, 40, 1.0)
        for h in range(2):
            new = 0.2 * v[h] + rhs[x, h, 8:40, :] + gain[x, h, 8:40, :] * s[h]
            pot[x - 4, :, 128 * h : 128 * h + 128] = new
        return carry

    for k in range(4):
        lax.fori_loop(4 + 8 * k, 12 + 8 * k, one, 0, unroll=8)
        part = pl.ds(8 * k, 8)
        copies.append(pltpu.make_async_copy(pot.at[part], pot_out.at[part], sem.at[k]))
        copies[-1].start()
    for c in copies:
        c.wait()


def body(conc_old, phi_old, solid_pot, phase_label, iface_block, iface_owner):
    n_grp, n_dev = lax.axis_size("grp"), lax.axis_size("dev")
    fine = pltpu.VMEM((FX, 2, FY, 128), F32)
    mid = pltpu.VMEM((MX, 2, MY, 128), F32)
    coarse = pltpu.VMEM((GX, 2, GY, 128), F32)
    dma = pltpu.SemaphoreType.DMA
    out = jax.ShapeDtypeStruct(conc_old.shape, F32)
    kept = pltpu.VMEM(conc_old.shape, F32)
    hbm = pl.BlockSpec(memory_space=pltpu.HBM)
    vmem = pl.BlockSpec(memory_space=pltpu.VMEM)

    def faces(n, deep, dtype=F32):
        c = 8 * ((4 * deep + 7) // 8)
        return [pltpu.VMEM((2, 2, n * deep, 128), dtype), pltpu.VMEM((2, 2, n * deep + 2 * c, 128), dtype)]

    arguments = (conc_old, phi_old, solid_pot, phase_label, iface_owner.reshape(1, 256), iface_block)
    fields = pl.pallas_call(
        functools.partial(kernel, n_grp, n_dev),
        out_shape=(kept, kept, fine, fine, fine),
        in_specs=[hbm] * 6,
        out_specs=(vmem,) * 5,
        scratch_shapes=[
            fine, pltpu.VMEM((FX, 2, FY, 128), jnp.int32), fine, pltpu.VMEM((32, 2, 32, 128), F32),
            fine, fine, pltpu.VMEM((32, 2, 32, 128), F32), fine, fine, fine, fine, fine, fine,
            mid, mid, mid, mid, mid, mid, mid,
            coarse, coarse, coarse, coarse, coarse, coarse, coarse, coarse, coarse, coarse,
            pltpu.VMEM((EX, 2, EY, 128), F32),
            *faces(32, 4), *faces(32, 3, jnp.int32), *faces(32, 3), *faces(32, 2), *faces(32, 1),
            *faces(16, 2), *faces(16, 2), *faces(16, 3), *faces(8, 2),
            pltpu.VMEM((2, 2, 1, 128), jnp.int32), pltpu.VMEM((n_dev, 1, 128), jnp.int32), pltpu.VMEM((n_dev, 1, 128), jnp.int32), pltpu.VMEM((64, 4096), F32),
            pltpu.VMEM((2, 128), F32), pltpu.VMEM((n_dev, 2, 128), F32), pltpu.VMEM((3, 8, 128), F32),
            dma((12,)), dma((9, 8)), dma((9, 8)), dma((2, 2)), dma((2, 2)),
            dma((n_dev,)), dma((n_dev,)), dma((n_dev,)), dma((n_dev,)), dma((2,)), dma((2,)),
        ],
        compiler_params=pltpu.CompilerParams(
            collective_id=0, has_side_effects=True, vmem_limit_bytes=43 * 1024 * 1024
        ),
    )(*[pltpu.with_memory_space_constraint(argument, pltpu.HBM) for argument in arguments])
    return pl.pallas_call(
        finish,
        out_shape=(out, out, out),
        in_specs=[vmem] * 5,
        out_specs=(hbm, hbm, hbm),
        scratch_shapes=[pltpu.VMEM(conc_old.shape, F32), dma((6,))],
        compiler_params=pltpu.CompilerParams(vmem_limit_bytes=8 * 1024 * 1024),
    )(*[pltpu.with_memory_space_constraint(field, pltpu.VMEM) for field in fields])


def solution(mesh):
    split = P("grp", "dev", None)
    return jax.shard_map(
        body,
        mesh=mesh,
        in_specs=(split, split, split, split, P("grp", "dev"), split),
        out_specs=(split, split, split),
        check_vma=False,
    )
```

```python
import functools

import jax
import jax.numpy as jnp
from jax import lax
from jax.experimental import pallas as pl
from jax.experimental.pallas import tpu as pltpu
from jax.sharding import PartitionSpec as P

MESH = pl.DeviceIdType.MESH
F32 = jnp.float32

FX, FY = 40, 48
MX, MY = 24, 32
EX, EY = 16, 24
GX, GY = 10, 40


def lookup(label, table):
    return jnp.where(label == 0, table[0], jnp.where(label == 1, table[1], table[2])).astype(F32)


def z_sum(a, b):
    lane = lax.broadcasted_iota(jnp.int32, (1, 128), 1)
    l0, l1 = lane == 0, lane == 127
    ra, rb = pltpu.roll(a, 1, 1), pltpu.roll(b, 1, 1)
    sa, sb = pltpu.roll(a, 127, 1), pltpu.roll(b, 127, 1)
    zero = jnp.zeros_like(a)
    za = jnp.where(l0, zero, ra) + jnp.where(l1, sb, sa)
    zb = jnp.where(l0, ra, rb) + jnp.where(l1, zero, sb)
    return za, zb


def plane(field, x, h, r0, r1):
    return (field[x - 1, h, r0:r1, :] + field[x + 1, h, r0:r1, :]) + (
        field[x, h, r0 - 1 : r1 - 1, :] + field[x, h, r0 + 1 : r1 + 1, :]
    )


def stencil(field, x, r0, r1, weight):
    a, b = field[x, 0, r0:r1, :], field[x, 1, r0:r1, :]
    za, zb = z_sum(a, b)
    pa, pb = plane(field, x, 0, r0, r1), plane(field, x, 1, r0, r1)
    if weight != 1.0:
        pa, pb = weight * pa, weight * pb
    return (a, b), (pa + za, pb + zb)


def kernel(
    n_grp,
    n_dev,
    conc_hbm,
    phi_hbm,
    solid_hbm,
    label_hbm,
    owner_hbm,
    block_hbm,
    conc_out,
    flux_out,
    ca,
    gg,
    bb,
    c0, lb, ph, sp, cb, cd, rs, dd, cc, kk, qq, fx, p2,
    sm, km, gm, bm, m1, m2, mu,
    kc, rc, gc, wa, wb, ka, kb, sc, ea, eb,
    ec,
    ysc, yrc, ysl, yrl, ysp, yrp, ysf, yrf, ysu, yru, ysk, yrk, yss, yrs, ysm, yrm, yse, yre,
    lists, lsend, lrecv, msk, psend, precv, shifts,
    in_sem, hs_sem, hr_sem, cs_sem, cr_sem, ls_sem, lr_sem, ps_sem, pr_sem, ss_sem, sr_sem,
):
    g = lax.axis_index("grp")
    d = lax.axis_index("dev")
    gu, gd = lax.rem(g + 1, n_grp), lax.rem(g + n_grp - 1, n_grp)
    du, dl = lax.rem(d + 1, n_dev), lax.rem(d + n_dev - 1, n_dev)
    eight = [(gd, dl), (gd, d), (gd, du), (g, dl), (g, du), (gu, dl), (gu, d), (gu, du)]

    loads = []
    for k, (src, dst) in enumerate(((conc_hbm, c0), (label_hbm, lb), (phi_hbm, ph))):
        for h in range(2):
            loads.append(
                pltpu.make_async_copy(
                    src.at[:, :, pl.ds(128 * h, 128)], dst.at[pl.ds(4, 32), h, pl.ds(8, 32), :], in_sem.at[2 * k + h]
                )
            )
    for h in range(2):
        loads.append(
            pltpu.make_async_copy(solid_hbm.at[:, :, pl.ds(128 * h, 128)], sp.at[:, h], in_sem.at[6 + h])
        )
    for k, src in enumerate((owner_hbm, block_hbm)):
        for r in range(2):
            loads.append(
                pltpu.make_async_copy(src.at[:, pl.ds(128 * r, 128)], lists.at[k, r], in_sem.at[8 + 2 * k + r])
            )
    for load in loads:
        load.start()

    barrier = pltpu.get_barrier_semaphore()
    for t in (eight[0], eight[1], eight[2], eight[5], eight[6], eight[7]):
        pl.semaphore_signal(barrier, inc=1, device_id=t, device_id_type=MESH)

    def greet(j, carry):
        pl.semaphore_signal(barrier, inc=1, device_id=(g, lax.rem(d + j, n_dev)), device_id_type=MESH)
        return carry

    lax.fori_loop(1, n_dev, greet, 0)

    for ref, rows in ((kc, (0, 8, 32, 40)), (sc, (0, 8, 32, 40)), (ka, (0, 8, 32, 40)), (kb, (0, 8, 32, 40)), (ea, (0, 8, 32, 40)), (eb, (0, 8, 32, 40))):
        ref[:, :, 0:8, :] = jnp.zeros((GX, 2, 8, 128), F32)
        ref[:, :, 32:40, :] = jnp.zeros((GX, 2, 8, 128), F32)
        ref[0] = jnp.zeros((2, GY, 128), F32)
        ref[GX - 1] = jnp.zeros((2, GY, 128), F32)

    def pack(field, ys, n, deep, off=0):
        def one(x, carry):
            for s, r in ((0, 8 + off), (1, 8 + n - deep - off)):
                for h in range(2):
                    ys[s, h, pl.ds(deep * x, deep), :] = field[4 + x, h, r : r + deep, :]
            return carry

        lax.fori_loop(0, n, one, 0, unroll=8)

    def unpack(field, yr, n, deep, wide, zero, off=0, corners=True):
        edge_rows = 8 * ((4 * deep + 7) // 8)

        def one(x, carry):
            for s, r, edge in ((0, 8 - deep - off, d == 0), (1, 8 + n + off, d == n_dev - 1)):
                for h in range(2):
                    v = yr[s, h, pl.ds(edge_rows + deep * (x - 4), deep), :]
                    field[x, h, r : r + deep, :] = jnp.where(edge, jnp.zeros_like(v), v)
            return carry

        reach = wide if corners else 0
        lax.fori_loop(4 - reach, 4 + n + reach, one, 0, unroll=8)
        if zero:
            @pl.when(g == 0)
            def _():
                field[4 - wide - off : 4 - off] = jnp.zeros(field.at[4 - wide : 4].shape, field.dtype)

            @pl.when(g == n_grp - 1)
            def _():
                field[4 + n + off : 4 + n + wide + off] = jnp.zeros(field.at[4 - wide : 4].shape, field.dtype)

    def halo(e, field, ys, yr, n, deep, wide, off=0, corners=True):
        c = 8 * ((4 * deep + 7) // 8)
        m = n * deep
        own = pl.ds(8, n)
        low, high = field.at[pl.ds(4 + off, wide), :, own, :], field.at[pl.ds(4 + n - wide - off, wide), :, own, :]
        to_low, to_high = field.at[pl.ds(4 - wide - off, wide), :, own, :], field.at[pl.ds(4 + n + off, wide), :, own, :]
        first, last, after, before = pl.ds(0, c), pl.ds(m - c, c), pl.ds(c + m, c), pl.ds(0, c)
        pairs = [
            (ys.at[0, :, first], yr.at[1, :, after]),
            (low, to_high),
            (ys.at[1, :, first], yr.at[0, :, after]),
            (ys.at[0], yr.at[1, :, pl.ds(c, m)]),
            (ys.at[1], yr.at[0, :, pl.ds(c, m)]),
            (ys.at[0, :, last], yr.at[1, :, before]),
            (high, to_low),
            (ys.at[1, :, last], yr.at[0, :, before]),
        ]
        copies = []
        for i in (0, 2, 5, 7, 4, 3, 6, 1) if corners else (4, 3, 6, 1):
            src, dst = pairs[i]
            copies.append(
                pltpu.make_async_remote_copy(
                    src_ref=src, dst_ref=dst, send_sem=hs_sem.at[e, i], recv_sem=hr_sem.at[e, i],
                    device_id=eight[i], device_id_type=MESH,
                )
            )
        for c in copies:
            c.start()
        return copies

    def sent(copies):
        for c in copies:
            c.wait_send()

    def arrive(copies):
        for c in copies:
            c.wait_recv()

    def all_send(src, dst, send_sem, recv_sem):
        def one(j, carry):
            pltpu.make_async_remote_copy(
                src_ref=src.at[lax.rem(d + j, n_dev)] if src.shape[0] == n_dev else src, dst_ref=dst.at[d], send_sem=send_sem.at[j], recv_sem=recv_sem.at[d],
                device_id=(g, lax.rem(d + j, n_dev)), device_id_type=MESH,
            ).start()
            return carry

        lax.fori_loop(1, n_dev, one, 0)

    def all_wait(src, dst, send_sem, recv_sem):
        def one(j, carry):
            s = lax.rem(d + n_dev - j, n_dev)
            c = pltpu.make_async_remote_copy(
                src_ref=src.at[lax.rem(d + j, n_dev)] if src.shape[0] == n_dev else src, dst_ref=dst.at[s], send_sem=send_sem.at[j], recv_sem=recv_sem.at[s],
                device_id=(g, lax.rem(d + j, n_dev)), device_id_type=MESH,
            )
            c.wait_recv()
            c.wait_send()
            return carry

        lax.fori_loop(1, n_dev, one, 0)

    def sweep(src, dst, gain, rhs, x0, x1, r0, r1, weight, unroll):
        def one(x, carry):
            v, s = stencil(src, x, r0, r1, weight)
            for h in range(2):
                dst[x, h, r0:r1, :] = 0.2 * v[h] + rhs[x, h, r0:r1, :] + gain[x, h, r0:r1, :] * s[h]
            return carry

        lax.fori_loop(x0, x1, one, 0, unroll=unroll)

    for k in range(4):
        loads[k].wait()
    pack(c0, ysc, 32, 4)
    pack(lb, ysl, 32, 3)

    def conc_coeffs(x, r0, r1):
        for h in range(2):
            old = c0[x, h, r0:r1, :]
            label = lb[x, h, r0:r1, :]
            dd[x, h, r0:r1, :] = jnp.where(old > 0.0, lookup(label, (1.5 / 10.0, 0.1 / 1.6, 0.4 / 3.4)), 0.0)
            cc[x, h, r0:r1, :] = old * lookup(label, (1.0 / 10.0, 1.0 / 1.6, 1.0 / 3.4))

    def pot_coeffs(x, r0, r1):
        for h in range(2):
            con = lookup(lb[x, h, r0:r1, :], (1.0, 0.3, 0.6)) * c0[x, h, r0:r1, :]
            rd = 0.8 / (0.05 + 6.0 * con)
            kk[x, h, r0:r1, :] = con
            bb[x, h, r0:r1, :] = rd
            gg[x, h, r0:r1, :] = rd * con

    def each(lo, hi, unroll, *fns):
        def one(x, carry):
            for fn in fns:
                fn(x)
            return carry

        lax.fori_loop(lo, hi, one, 0, unroll=unroll)

    each(4, 36, 4, lambda x: conc_coeffs(x, 8, 40), lambda x: pot_coeffs(x, 8, 40))
    loads[4].wait()
    loads[5].wait()
    pack(ph, ysp, 32, 3)
    for k in range(8, 12):
        loads[k].wait()
    owners = jnp.concatenate([lists[0, 0], lists[0, 1]], axis=1)
    values = jnp.concatenate([lists[1, 0], lists[1, 1]], axis=1) + 1
    onehot = lax.broadcasted_iota(jnp.int32, (n_dev, 256), 0) == owners
    ones = jnp.where(onehot, 1.0, 0.0)
    earlier = lax.broadcasted_iota(jnp.int32, (256, 256), 0) < lax.broadcasted_iota(jnp.int32, (256, 256), 1)
    before = jnp.dot(
        ones.astype(jnp.bfloat16), jnp.where(earlier, 1.0, 0.0).astype(jnp.bfloat16), preferred_element_type=F32
    )
    rank = jnp.sum(ones * before, axis=0, keepdims=True) + (16 * lax.rem(d, 8)).astype(F32)
    slots = lax.broadcasted_iota(jnp.int32, (128, 256), 0).astype(F32) == rank
    slots = jnp.where(slots, 1.0, 0.0).astype(jnp.bfloat16)
    by_owner = jnp.zeros((n_dev, 128), F32)
    for part, scale in ((values >> 6, 64.0), (values & 63, 1.0)):
        terms = jnp.where(onehot, part.astype(F32), 0.0).astype(jnp.bfloat16)
        by_owner = by_owner + scale * lax.dot_general(
            terms, slots, (((1,), (1,)), ((), ())), preferred_element_type=F32
        )
    by_owner = by_owner.astype(jnp.int32) - 1
    for o in range(n_dev):
        lsend[o] = by_owner[o : o + 1, :]
    lrecv[d] = lsend[d]

    def own_mid(i, carry):
        for h in range(2):
            total = jnp.zeros((16, 128), F32)
            for x in (0, 1):
                for r in (0, 1):
                    rows = pl.ds(8 + r, 16, stride=2)
                    total = total + kk[4 + 2 * i + x, h, rows, :]
            km[4 + i, h, 8:24, :] = 0.25 * total
        return carry

    lax.fori_loop(0, 16, own_mid, 0, unroll=4)
    pack(km, ysk, 16, 2)

    def own_coarse(dst, src, off):
        def one(i, carry):
            for h in range(2):
                total = jnp.zeros((8, 128), F32)
                for x in (0, 1):
                    for r in (0, 1):
                        total = total + src[off + 2 * i + x, h, pl.ds(8 + r, 8, stride=2), :]
                dst[1 + i, h, 16:24, :] = 0.25 * total
            return carry

        lax.fori_loop(0, 8, one, 0, unroll=8)

    def coarse_exchange(field, k):
        copies = []
        for i, (t, r) in enumerate((((g, dl), 24), ((g, du), 8))):
            copies.append(
                pltpu.make_async_remote_copy(
                    src_ref=field.at[pl.ds(1, 8), :, pl.ds(16, 8), :], dst_ref=field.at[pl.ds(1, 8), :, pl.ds(r, 8), :],
                    send_sem=cs_sem.at[k, i], recv_sem=cr_sem.at[k, i], device_id=t, device_id_type=MESH,
                )
            )
        for c in copies:
            c.start()
        return copies

    def coarse_edges(field):
        @pl.when(d == 0)
        def _():
            field[:, :, 8:16, :] = jnp.zeros((GX, 2, 8, 128), F32)

        @pl.when(d == n_dev - 1)
        def _():
            field[:, :, 24:32, :] = jnp.zeros((GX, 2, 8, 128), F32)

    own_coarse(kc, km, 4)

    pl.semaphore_wait(barrier, n_dev - 1 + 6)
    all_send(lsend, lrecv, ls_sem, lr_sem)
    h_conc = halo(0, c0, ysc, yrc, 32, 4, 4)
    h_label = halo(1, lb, ysl, yrl, 32, 3, 3)

    def conc_at(src, dst, x, r0, r1):
        _, s = stencil(src, x, r0, r1, 1.0)
        for h in range(2):
            v = cc[x, h, r0:r1, :] + dd[x, h, r0:r1, :] * s[h]
            if dst is None:
                conc_out[x - 4, r0 - 8 : r1 - 8, 128 * h : 128 * h + 128] = v
            else:
                dst[x, h, r0:r1, :] = v

    steps = ((c0, ca), (ca, cb), (cb, cd), (cd, None))
    for k, (src, dst) in enumerate(steps):
        each(5 + k, 35 - k, 15 - k, lambda x, src=src, dst=dst: conc_at(src, dst, x, 8, 40))
    for k in (6, 7):
        loads[k].wait()
    all_wait(lsend, lrecv, ls_sem, lr_sem)

    counts = jnp.zeros((64, 32), F32)
    for q in range(n_dev // 8):
        block = lrecv[8 * q]
        for k in range(1, 8):
            block = jnp.maximum(block, lrecv[8 * q + k])
        place = jnp.where(block >= 0, (block & 1) * 32 + ((block >> 1) & 31), -1)
        rows = jnp.where(lax.broadcasted_iota(jnp.int32, (64, 128), 0) == place, 1.0, 0.0).astype(jnp.bfloat16)
        cols = jnp.where(lax.broadcasted_iota(jnp.int32, (32, 128), 0) == block >> 6, 1.0, 0.0).astype(jnp.bfloat16)
        counts = counts + lax.dot_general(rows, cols, (((1,), (1,)), ((), ())), preferred_element_type=F32)
    named = jnp.where(counts > 0.0, 1.0, 0.0).astype(jnp.bfloat16)
    spread = (
        lax.broadcasted_iota(jnp.int32, (32, 4096), 1) // 128 == lax.broadcasted_iota(jnp.int32, (32, 4096), 0)
    ).astype(jnp.bfloat16)
    msk[...] = jnp.dot(named, spread, preferred_element_type=F32)
    arrive(h_conc)
    unpack(c0, yrc, 32, 4, 4, True)
    arrive(h_label)
    unpack(lb, yrl, 32, 3, 3, False)
    h_phi = halo(2, ph, ysp, yrp, 32, 3, 3)
    each(1, 4, 3, lambda x: conc_coeffs(x, 0, 48), lambda x: conc_coeffs(x + 35, 0, 48))
    each(4, 36, 32, lambda x: conc_coeffs(x, 0, 8), lambda x: conc_coeffs(x, 40, 48))
    for k, (src, dst) in enumerate(steps):
        r0, r1, low, high = (4, 44, (4, 12), (36, 44)) if k < 3 else (8, 40, (8, 16), (32, 40))
        each(
            1 + k, 5 + k, 4,
            lambda x, src=src, dst=dst, r0=r0, r1=r1: conc_at(src, dst, x, r0, r1),
            lambda x, src=src, dst=dst, r0=r0, r1=r1, k=k: conc_at(src, dst, x + 34 - 2 * k, r0, r1),
        )
        each(
            5 + k, 35 - k, 30 - 2 * k,
            lambda x, src=src, dst=dst, low=low: conc_at(src, dst, x, *low),
            lambda x, src=src, dst=dst, high=high: conc_at(src, dst, x, *high),
        )

    def flux_at(x, r0, r1):
        for h in range(2):
            con = conc_out[x, r0:r1, 128 * h : 128 * h + 128]
            u = 0.5 * (sp[x, h, r0:r1, :] - ph[4 + x, h, 8 + r0 : 8 + r1, :]) - 0.1 * jnp.log(con)
            kin = lookup(lb[4 + x, h, 8 + r0 : 8 + r1, :], (0.2, 1.0, 0.5)) * jnp.sqrt(con)
            val = kin * (jnp.exp(u) - jnp.exp(-u))
            val = msk[32 * h + r0 : 32 * h + r1, 128 * x : 128 * x + 128] * val
            fx[4 + x, h, 8 + r0 : 8 + r1, :] = val
            flux_out[x, r0:r1, 128 * h : 128 * h + 128] = val

    for x in range(32):
        if x in (0, 1, 30, 31):
            flux_at(x, 0, 32)
        else:
            flux_at(x, 0, 8)
            flux_at(x, 24, 32)
    pack(fx, ysf, 32, 2)
    h_flux = halo(4, fx, ysf, yrf, 32, 2, 2)
    for x in range(2, 30):
        flux_at(x, 8, 24)

    each(2, 4, 2, lambda x: pot_coeffs(x, 0, 48), lambda x: pot_coeffs(x + 34, 0, 48))
    each(4, 36, 8, lambda x: pot_coeffs(x, 0, 8), lambda x: pot_coeffs(x, 40, 48))
    arrive(h_phi)
    unpack(ph, yrp, 32, 3, 3, True)

    def first(x, carry):
        v, s = stencil(ph, x, 4, 44, 1.0)
        for h in range(2):
            rd = bb[x, h, 4:44, :]
            qq[x, h, 4:44, :] = (0.2 + 0.05 * rd) * v[h] + gg[x, h, 4:44, :] * s[h]
        return carry

    lax.fori_loop(2, 38, first, 0, unroll=12)

    def second(x, r0, r1):
        for h in range(2):
            rd = bb[x, h, r0:r1, :]
            fl = fx[x, h, r0:r1, :]
            ca[x, h, r0:r1, :] = qq[x, h, r0:r1, :] + rd * fl
            src = 0.05 * ph[x, h, r0:r1, :] + fl
            qq[x, h, r0:r1, :] = src
            bb[x, h, r0:r1, :] = rd * src

    def smooth(x, r0, r1):
        v, s = stencil(ca, x, r0, r1, 1.0)
        for h in range(2):
            p2[x, h, r0:r1, :] = 0.2 * v[h] + bb[x, h, r0:r1, :] + gg[x, h, r0:r1, :] * s[h]

    def resid(x, r0, r1):
        v, s = stencil(p2, x, r0, r1, 1.0)
        for h in range(2):
            rs[x - 4, h, r0 - 8 : r1 - 8, :] = (
                qq[x, h, r0:r1, :] - 0.05 * v[h] - kk[x, h, r0:r1, :] * (6.0 * v[h] - s[h])
            )

    each(4, 36, 8, lambda x: second(x, 8, 40))
    each(5, 35, 15, lambda x: smooth(x, 8, 40))
    each(6, 34, 14, lambda x: resid(x, 8, 40))
    h_km = halo(3, km, ysk, yrk, 16, 2, 2)
    x_kc = coarse_exchange(kc, 0)
    arrive(h_flux)
    unpack(fx, yrf, 32, 2, 2, True)
    each(2, 4, 2, lambda x: second(x, 4, 44), lambda x: second(x + 34, 4, 44))
    each(4, 36, 32, lambda x: second(x, 0, 8), lambda x: second(x, 40, 48))
    each(3, 5, 2, lambda x: smooth(x, 4, 44), lambda x: smooth(x + 32, 4, 44))
    each(5, 35, 30, lambda x: smooth(x, 4, 12), lambda x: smooth(x, 36, 44))
    each(4, 6, 2, lambda x: resid(x, 8, 40), lambda x: resid(x + 30, 8, 40))
    each(6, 34, 28, lambda x: resid(x, 8, 16), lambda x: resid(x, 32, 40))

    def down(i, carry):
        for h in range(2):
            total = jnp.zeros((16, 128), F32)
            for x in (0, 1):
                for r in (0, 1):
                    total = total + rs[2 * i + x, h, pl.ds(r, 16, stride=2), :]
            sm[4 + i, h, 8:24, :] = 0.25 * total
        return carry

    lax.fori_loop(0, 16, down, 0, unroll=16)
    pack(sm, yss, 16, 2)
    h_sm = halo(5, sm, yss, yrs, 16, 2, 2)
    pack(p2, ysu, 32, 1, 1)
    arrive(h_km)
    unpack(km, yrk, 16, 2, 2, True)

    def mid_coeffs(x, carry):
        for h in range(2):
            con = km[x, h, 4:28, :]
            rd = 0.8 / (0.05 + 3.0 * con)
            bm[x, h, 4:28, :] = rd
            gm[x, h, 4:28, :] = rd * con
        return carry

    lax.fori_loop(2, 22, mid_coeffs, 0, unroll=5)
    h_p2 = halo(7, p2, ysu, yru, 32, 1, 1, 1, False)
    arrive(x_kc)
    coarse_edges(kc)

    def coarse_coeffs(x, carry):
        for h in range(2):
            con = kc[x, h, 8:32, :]
            rd = 0.8 / (0.05 + 2.25 * con)
            rc[x, h, 8:32, :] = rd
            gc[x, h, 8:32, :] = rd * con
            wa[x, h, 8:32, :] = jnp.ones((24, 128), F32)
            ka[x, h, 8:32, :] = con
        return carry

    lax.fori_loop(1, 9, coarse_coeffs, 0, unroll=4)

    def dual(w_in, k_in, w_out, k_out):
        def one(x, carry):
            v, s = stencil(k_in, x, 8, 32, 0.0625)
            for h in range(2):
                w = w_in[x, h, 8:32, :]
                w = w - rc[x, h, 8:32, :] * (0.05 * w + 2.25 * v[h] - s[h])
                w_out[x, h, 8:32, :] = w
                k_out[x, h, 8:32, :] = kc[x, h, 8:32, :] * w
            return carry

        lax.fori_loop(1, 9, one, 0, unroll=8)

    for k in range(4):
        dual(wa, ka, wb, kb)
        dual(wb, kb, wa, ka)

    load = jnp.zeros((8, 128), F32)
    row = lax.broadcasted_iota(jnp.int32, (8, 128), 0)
    lane8 = lax.broadcasted_iota(jnp.int32, (8, 128), 1)
    edge_y = jnp.where(((row == 0) & (d == 0)) | ((row == 7) & (d == n_dev - 1)), 1.0, 0.0)
    for x in range(8):
        for h in range(2):
            edge_z = jnp.where(lane8 == 127 * h, 1.0, 0.0)
            edge_xy = edge_y + (1.0 if x in (0, 7) else 0.0)
            load = load + (0.05 + kc[1 + x, h, 16:24, :] * (0.0625 * edge_xy + edge_z))
    load = jnp.sum(load, axis=0, keepdims=True)
    row2 = lax.broadcasted_iota(jnp.int32, (2, 128), 0)

    arrive(h_sm)
    unpack(sm, yrs, 16, 2, 2, True)

    def mid_first(x, carry):
        for h in range(2):
            v = bm[x, h, 4:28, :] * sm[x, h, 4:28, :]
            bm[x, h, 4:28, :] = v
            m1[x, h, 4:28, :] = v
        return carry

    lax.fori_loop(2, 22, mid_first, 0, unroll=20)
    sweep(m1, m2, gm, bm, 3, 21, 4, 28, 0.25, 18)

    def mid_resid(x, carry):
        v, s = stencil(m2, x, 8, 24, 0.25)
        for h in range(2):
            m1[x, h, 8:24, :] = sm[x, h, 8:24, :] - 0.05 * v[h] - km[x, h, 8:24, :] * (3.0 * v[h] - s[h])
            mu[x, h, 8:24, :] = v[h]
        return carry

    lax.fori_loop(4, 20, mid_resid, 0, unroll=16)

    own_coarse(sc, m1, 4)
    x_sc = coarse_exchange(sc, 1)
    part = jnp.zeros((8, 128), F32)
    for x in range(8):
        for h in range(2):
            part = part + wa[1 + x, h, 16:24, :] * sc[1 + x, h, 16:24, :]
    part = jnp.sum(part, axis=0, keepdims=True)
    message = jnp.where(row2 == 0, jnp.broadcast_to(part, (2, 128)), jnp.broadcast_to(load, (2, 128)))
    psend[...] = message
    precv[d] = message
    all_send(psend, precv, ps_sem, pr_sem)
    pack(mu, ysm, 16, 3)
    arrive(x_sc)
    coarse_edges(sc)
    h_mu = halo(8, mu, ysm, yrm, 16, 3, 3)

    def coarse_first(x, carry):
        for h in range(2):
            v = rc[x, h, 8:32, :] * sc[x, h, 8:32, :]
            rc[x, h, 8:32, :] = v
            ea[x, h, 8:32, :] = v
        return carry

    lax.fori_loop(1, 9, coarse_first, 0, unroll=8)
    for k in range(3):
        sweep(ea, eb, gc, rc, 1, 9, 8, 32, 0.0625, 8)
        sweep(eb, ea, gc, rc, 1, 9, 8, 32, 0.0625, 8)
    sweep(ea, eb, gc, rc, 1, 9, 8, 32, 0.0625, 8)
    for x in range(8):
        for h in range(2):
            ec[4 + x, h, 8:16, :] = eb[1 + x, h, 16:24, :]
    pack(ec, yse, 8, 2)
    h_ec = halo(6, ec, yse, yre, 8, 2, 2)
    all_wait(psend, precv, ps_sem, pr_sem)

    def gather(s, carry):
        return carry + precv[s]

    sums = lax.fori_loop(0, n_dev, gather, jnp.zeros((2, 128), F32), unroll=8)
    sums = jnp.sum(sums, axis=1, keepdims=True)
    shifts[1] = jnp.broadcast_to(sums[0:1] / sums[1:2], (8, 128))
    x_shift = []
    for k, (t, i) in enumerate((((gd, d), 2), ((gu, d), 0))):
        x_shift.append(
            pltpu.make_async_remote_copy(
                src_ref=shifts.at[1], dst_ref=shifts.at[i], send_sem=ss_sem.at[k], recv_sem=sr_sem.at[k],
                device_id=t, device_id_type=MESH,
            )
        )
    for c in x_shift:
        c.start()
    arrive(h_mu)
    sent(h_mu)
    unpack(mu, yrm, 16, 3, 3, True)
    arrive(h_p2)
    sent(h_p2)
    unpack(p2, yru, 32, 1, 1, True, 1, False)
    arrive(h_ec)
    unpack(ec, yre, 8, 2, 2, True)
    arrive(x_shift)

    row12 = lax.broadcasted_iota(jnp.int32, (12, 128), 0)
    inside = jnp.where(((row12 < 2) & (d == 0)) | ((row12 >= 10) & (d == n_dev - 1)), 0.0, 1.0)
    own_shift = inside * shifts[1, 0:1, :]
    low_shift = jnp.where(g == 0, jnp.zeros((12, 128), F32), inside * shifts[0, 0:1, :])
    high_shift = jnp.where(g == n_grp - 1, jnp.zeros((12, 128), F32), inside * shifts[2, 0:1, :])
    for i in range(2, 14):
        for h in range(2):
            v = ec[i, h, 6:18, :] + (low_shift if i < 4 else own_shift if i < 12 else high_shift)
            for x in (0, 1):
                if not 1 <= 2 * i - 4 + x < 23:
                    continue
                for r in (0, 1):
                    rows = pl.ds(4 + r, 12, stride=2)
                    mu[2 * i - 4 + x, h, rows, :] = mu[2 * i - 4 + x, h, rows, :] + v
    sweep(mu, m1, gm, bm, 2, 22, 4, 28, 0.25, 20)
    sweep(m1, m2, gm, bm, 3, 21, 4, 28, 0.25, 18)

    def fine_up(i, carry):
        for h in range(2):
            v = m2[i, h, 6:26, :]
            for x in (0, 1):
                for r in (0, 1):
                    rows = pl.ds(4 + r, 20, stride=2)
                    p2[2 * i - 4 + x, h, rows, :] = p2[2 * i - 4 + x, h, rows, :] + v
        return carry

    lax.fori_loop(3, 21, fine_up, 0, unroll=18)
    sweep(p2, ca, gg, bb, 3, 37, 4, 44, 1.0, 34)

    for copies in (h_conc, h_label, h_phi, h_km, h_flux, h_sm, h_ec, x_kc, x_sc, x_shift):
        sent(copies)


def finish(conc, flux, last, gain, rhs, conc_out, flux_out, pot_out, pot, sem):
    copies = [pltpu.make_async_copy(conc, conc_out, sem.at[4]), pltpu.make_async_copy(flux, flux_out, sem.at[5])]
    for c in copies:
        c.start()

    def one(x, carry):
        v, s = stencil(last, x, 8, 40, 1.0)
        for h in range(2):
            new = 0.2 * v[h] + rhs[x, h, 8:40, :] + gain[x, h, 8:40, :] * s[h]
            pot[x - 4, :, 128 * h : 128 * h + 128] = new
        return carry

    for k in range(4):
        lax.fori_loop(4 + 8 * k, 12 + 8 * k, one, 0, unroll=8)
        part = pl.ds(8 * k, 8)
        copies.append(pltpu.make_async_copy(pot.at[part], pot_out.at[part], sem.at[k]))
        copies[-1].start()
    for c in copies:
        c.wait()


def body(conc_old, phi_old, solid_pot, phase_label, iface_block, iface_owner):
    n_grp, n_dev = lax.axis_size("grp"), lax.axis_size("dev")
    fine = pltpu.VMEM((FX, 2, FY, 128), F32)
    mid = pltpu.VMEM((MX, 2, MY, 128), F32)
    coarse = pltpu.VMEM((GX, 2, GY, 128), F32)
    dma = pltpu.SemaphoreType.DMA
    out = jax.ShapeDtypeStruct(conc_old.shape, F32)
    kept = pltpu.VMEM(conc_old.shape, F32)
    hbm = pl.BlockSpec(memory_space=pltpu.HBM)
    vmem = pl.BlockSpec(memory_space=pltpu.VMEM)

    def faces(n, deep, dtype=F32):
        c = 8 * ((4 * deep + 7) // 8)
        return [pltpu.VMEM((2, 2, n * deep, 128), dtype), pltpu.VMEM((2, 2, n * deep + 2 * c, 128), dtype)]

    arguments = (conc_old, phi_old, solid_pot, phase_label, iface_owner.reshape(1, 256), iface_block)
    fields = pl.pallas_call(
        functools.partial(kernel, n_grp, n_dev),
        out_shape=(kept, kept, fine, fine, fine),
        in_specs=[hbm] * 6,
        out_specs=(vmem,) * 5,
        scratch_shapes=[
            fine, pltpu.VMEM((FX, 2, FY, 128), jnp.int32), fine, pltpu.VMEM((32, 2, 32, 128), F32),
            fine, fine, pltpu.VMEM((32, 2, 32, 128), F32), fine, fine, fine, fine, fine, fine,
            mid, mid, mid, mid, mid, mid, mid,
            coarse, coarse, coarse, coarse, coarse, coarse, coarse, coarse, coarse, coarse,
            pltpu.VMEM((EX, 2, EY, 128), F32),
            *faces(32, 4), *faces(32, 3, jnp.int32), *faces(32, 3), *faces(32, 2), *faces(32, 1),
            *faces(16, 2), *faces(16, 2), *faces(16, 3), *faces(8, 2),
            pltpu.VMEM((2, 2, 1, 128), jnp.int32), pltpu.VMEM((n_dev, 1, 128), jnp.int32), pltpu.VMEM((n_dev, 1, 128), jnp.int32), pltpu.VMEM((64, 4096), F32),
            pltpu.VMEM((2, 128), F32), pltpu.VMEM((n_dev, 2, 128), F32), pltpu.VMEM((3, 8, 128), F32),
            dma((12,)), dma((9, 8)), dma((9, 8)), dma((2, 2)), dma((2, 2)),
            dma((n_dev,)), dma((n_dev,)), dma((n_dev,)), dma((n_dev,)), dma((2,)), dma((2,)),
        ],
        compiler_params=pltpu.CompilerParams(
            collective_id=0, has_side_effects=True, vmem_limit_bytes=43 * 1024 * 1024
        ),
    )(*[pltpu.with_memory_space_constraint(argument, pltpu.HBM) for argument in arguments])
    return pl.pallas_call(
        finish,
        out_shape=(out, out, out),
        in_specs=[vmem] * 5,
        out_specs=(hbm, hbm, hbm),
        scratch_shapes=[pltpu.VMEM(conc_old.shape, F32), dma((6,))],
        compiler_params=pltpu.CompilerParams(vmem_limit_bytes=8 * 1024 * 1024),
    )(*[pltpu.with_memory_space_constraint(field, pltpu.VMEM) for field in fields])


def solution(mesh):
    split = P("grp", "dev", None)
    return jax.shard_map(
        body,
        mesh=mesh,
        in_specs=(split, split, split, split, P("grp", "dev"), split),
        out_specs=(split, split, split),
        check_vma=False,
    )
```
